32 devices in a mesh: grp: 4 (over x, core), pen: 8 (over z, y).
Axes of the slice: x: 2, y: 2, z: 4, core: 2. Of those that a mesh axis runs over, the one named last changes fastest.
Arguments:
- u_field: float32 [2, 2048, 2048], P(None, ('grp', 'pen')), may hold values from -6 to 6
- v_field: float32 [2, 2048, 2048], P(None, ('grp', 'pen')), may hold values from -6 to 6
- ky_order: int32 [2048], replicated, may hold values from 0 to 2047, as said below
Outputs:
- deriv: float32 [2048, 2, 2, 2048], P('grp', None, None, 'pen')
The draws below stay inside these ranges and needn't reach their ends.
Inputs may be any that keep to these rules, and one draw needn't show every extreme that they name: ky_order is a permutation of 0 to 2047; for every position j, ky_order[2047 - j] = (2048 - ky_order[j]) mod 2048, except for the one pair of positions that holds 0 and 1024.
All inputs are finite; a program needn't handle non-finite values.
Results may differ from the reference program's by a relative error of at most 0.00007.
Values sent between devices are 32-bit elements; how exact they have to be, the bound alone decides.
No kernel may reach another device: no remote copies, remote signals or barrier semaphores. Data moves between devices by JAX's collectives and lax.ppermute only.
A program may use at most 64 MiB of HBM per device.

```python
import jax
import jax.numpy as jnp
from jax import lax

PLANES = 2
NY = 2048
NZ = 2048


def draw_ky_order(key, part):
    half_length = NY // 2
    order_key = jax.random.fold_in(key, 11)
    side_key = jax.random.fold_in(key, 23)
    pair_index = jax.random.permutation(order_key, half_length).astype(jnp.int32)
    side_flags = jax.random.randint(side_key, (half_length,), 0, 2)
    upper_value = jnp.where(pair_index > 0, NY - pair_index, half_length).astype(jnp.int32)
    first_half = jnp.where(side_flags > 0, upper_value, pair_index)
    second_half = jnp.where(side_flags > 0, pair_index, upper_value)
    return jnp.concatenate([first_half, second_half[::-1]]).astype(jnp.int32)


def shard_levels(key, extent, split, least, high):
    level = 1.0
    for axis_at, parts in split:
        draws = jax.random.uniform(jax.random.fold_in(jax.random.fold_in(key, 6), axis_at), (parts,), jnp.float32, least / len(split), high / len(split))
        level = level * jnp.repeat(jnp.exp(draws), extent[axis_at] // parts).reshape((-1,) + (1,) * (len(extent) - 1 - axis_at))
    return level


def gaussian(key, dims, deviation, bound, shards=(), kind=jnp.bfloat16):
    factor_of = shard_levels(key, dims, shards, -0.22, 0.18) if shards else 1.0
    entries = jax.random.normal(key, dims, jnp.float32) * deviation * factor_of
    return jnp.minimum(jnp.maximum(entries, -bound), bound).astype(kind)


def setup_inputs(seed: int = 0) -> dict:
    key_of = jax.random.split(jax.random.key(seed), 4)
    return {
        "u_field": gaussian(key_of[0], (PLANES, NZ, NY), 1.0, 6.0, ((1, 32),), jnp.float32),
        "v_field": gaussian(key_of[1], (PLANES, NZ, NY), 1.0, 6.0, ((1, 32),), jnp.float32),
        "ky_order": draw_ky_order(jax.random.fold_in(key_of[3], 71), 0),
    }


def signed_scale(length):
    waves = jnp.arange(length)
    signed = jnp.where(waves < length // 2, waves, waves - length)
    signed = jnp.where(waves == length // 2, 0, signed)
    return (2.0 / length) * signed.astype(jnp.float32)


def reference(u_field, v_field, ky_order):
    scale_y = signed_scale(NY)[None, :]
    scale_z = signed_scale(NZ)[:, None]

    def one_plane(pair):
        u_plane, v_plane = pair
        packed = u_plane + 1j * v_plane
        spectrum = jnp.fft.fft2(packed, axes=(0, 1), norm="ortho")
        mirror = jnp.conj(jnp.roll(jnp.flip(spectrum, (0, 1)), (1, 1), (0, 1)))
        first = 0.5 * (spectrum + mirror)
        second = -0.5j * (spectrum - mirror)
        combined = 1j * scale_y * first - scale_z * second
        field = jnp.fft.ifft(combined, axis=0, norm="ortho")
        field = jnp.take(field, ky_order, axis=1)
        return jnp.stack([jnp.real(field), jnp.imag(field)]).astype(jnp.float32)

    planes = lax.map(one_plane, (u_field, v_field))
    return jnp.transpose(planes, (2, 1, 0, 3))
```

```python
import functools
import math

import jax
import jax.numpy as jnp
import numpy as np
from jax import lax
from jax.experimental import pallas as pl
from jax.experimental.pallas import tpu as pltpu
from jax.sharding import PartitionSpec as P


f32 = jnp.float32
bf16 = jnp.bfloat16


def split_two(x):
    high = x.astype(bf16)
    return high, (x - high.astype(f32)).astype(bf16)


def split_three(x):
    high = x.astype(bf16)
    rest = x - high.astype(f32)
    middle = rest.astype(bf16)
    return high, middle, (rest - middle.astype(f32)).astype(bf16)


def dot(a, b):
    return jnp.dot(a, b, preferred_element_type=f32)


def signed_scale(waves, length):
    signed = jnp.where(waves < length // 2, waves, waves - length)
    signed = jnp.where(waves == length // 2, 0, signed)
    return 2.0 / length * signed.astype(f32)


def cos_sin(residue, length):
    eighth = length // 8
    turned = (residue + eighth) & (length - 1)
    turn = turned // (2 * eighth)
    x = (2.0 * math.pi / length) * (turned - turn * (2 * eighth) - eighth).astype(f32)
    y = x * x
    cosine = 1.0 + y * (-1 / 2 + y * (1 / 24 + y * (-1 / 720 + y * (1 / 40320))))
    sine = x * (1.0 + y * (-1 / 6 + y * (1 / 120 + y * (-1 / 5040 + y * (1 / 362880)))))
    odd = (turn & 1) == 1
    first, second = jnp.where(odd, sine, cosine), jnp.where(odd, cosine, sine)
    return (
        jnp.where((turn == 1) | (turn == 2), -first, first),
        jnp.where(turn >= 2, -second, second),
    )


def reverse_lanes(x, swap):
    high, middle, low = split_three(x)
    return dot(high, swap) + (dot(middle, swap) + dot(low, swap))


def transform_block(fields, table_ref, waves, first, slab):
    field_high, field_low = fields
    rows = field_high.shape[0] // 4
    half = table_ref.shape[2] // 2
    sums = []
    for part in range(2):
        columns = pl.ds(part * half + first, slab)
        high, low = table_ref[0, :, columns], table_ref[1, :, columns]
        sums.append(dot(field_high, high) + (dot(field_high, low) + dot(field_low, high)))
    residue = waves & 3
    sign = jnp.where((residue & 1) == 1, -1.0, 1.0)
    cosine = jnp.where(residue == 0, 1.0, jnp.where(residue == 2, -1.0, 0.0))
    sine = jnp.where(residue == 1, 1.0, jnp.where(residue == 3, -1.0, 0.0))

    def folded(x):
        return (
            x[:rows] + sign * x[2 * rows : 3 * rows],
            x[rows : 2 * rows] + sign * x[3 * rows :],
        )

    even_c, odd_c = folded(sums[0])
    even_s, odd_s = folded(sums[1])
    return (
        even_c + cosine * odd_c - sine * odd_s,
        even_s + cosine * odd_s + sine * odd_c,
    )


def fill_table(waves, table_ref):
    half = waves.shape[1]
    length = 2 * half
    norm = 1.0 / math.sqrt(length)
    fine = 32
    coarse = length // 4 // fine
    special = (waves == 0) | (waves == half)
    coarse_c, coarse_s = cos_sin(
        (fine * lax.broadcasted_iota(jnp.int32, (coarse, half), 0) * waves) & (length - 1), length
    )
    coarse_c, coarse_s = norm * coarse_c, norm * coarse_s
    index = lax.broadcasted_iota(jnp.int32, (fine, half), 0)
    fine_c, fine_s = cos_sin((index * waves) & (length - 1), length)
    other = norm * jnp.where((waves == 0) & ((index & 1) == 1), -1.0, 1.0)
    for a in range(coarse):
        this_c, this_s = coarse_c[a : a + 1], coarse_s[a : a + 1]
        here = slice(a * fine, (a + 1) * fine)
        cosines = this_c * fine_c - this_s * fine_s
        sines = this_c * fine_s + this_s * fine_c
        sines = jnp.where(special, other, sines)
        for part, values in enumerate((cosines, sines)):
            high, low = split_two(values)
            table_ref[0, here, part * half : (part + 1) * half] = high
            table_ref[1, here, part * half : (part + 1) * half] = low


def load_quarters(ref):
    quarter = ref.shape[1] // 4
    x = jnp.concatenate([ref[:, i * quarter : (i + 1) * quarter] for i in range(4)], 0)
    return split_two(x)


def second_kernel(sizes, order_ref, field_hbm, out_hbm, field_ref, table_ref, piece_ref, sems):
    planes, rows, slab, pens = sizes
    load = pltpu.make_async_copy(field_hbm, field_ref, sems.at[pens])
    load.start()
    half = order_ref.shape[1] // 2
    fill_table(order_ref[:, :half], table_ref)
    load.wait()
    fields = load_quarters(field_ref)
    copies = []
    for block in range(pens // 2):
        here = slice(block * slab, (block + 1) * slab)
        c, s = transform_block(fields, table_ref, order_ref[:, here], block * slab, slab)
        for part, values in enumerate((s, c)):
            for plane in range(planes):
                piece_ref[block, part * planes + plane] = values[plane * rows : (plane + 1) * rows]
        for target in (block, pens - 1 - block):
            copy = pltpu.make_async_copy(
                piece_ref.at[block], out_hbm.at[:, target], sems.at[target]
            )
            copy.start()
            copies.append(copy)
    for copy in copies:
        copy.wait()


def first_kernel(sizes, place_ref, order_ref, swap_ref, field_hbm, *refs):
    planes, rows, slab, pens = sizes
    outs, (field_ref, table_ref, piece_ref, sems) = refs[:pens], refs[pens:]
    load = pltpu.make_async_copy(field_hbm, field_ref, sems.at[pens])
    load.start()
    length = order_ref.shape[1]
    fill_table(order_ref[:, : length // 2], table_ref)
    load.wait()
    fields = load_quarters(field_ref)
    pen = place_ref[0]
    upper = pen >= pens // 2
    lanes = 128
    step = 2 * planes * (slab // lanes)
    copies = []
    for slot in range(pens // 2):
        target = pen ^ slot
        block = jnp.where(upper, pens - 1 - target, target)
        first = pl.multiple_of(block * slab, slab)
        waves = order_ref[:, pl.ds(first, slab)]
        c, s = transform_block(fields, table_ref, waves, first, slab)
        scale = signed_scale(waves, length)
        opposite = slot ^ (pens - 1)
        for part, values in enumerate((scale * s, scale * c)):
            turned = reverse_lanes(values, swap_ref[...])
            if part == 1:
                turned = -turned
            near, far = jnp.where(upper, turned, values), jnp.where(upper, values, turned)
            for to, piece in ((slot, near), (opposite, far)):
                for plane in range(planes):
                    for tile in range(slab // lanes):
                        at = (part * (slab // lanes) + tile) * planes + plane
                        piece_ref[to, pl.ds(at, rows, stride=step), :] = piece[
                            plane * rows : (plane + 1) * rows, tile * lanes : (tile + 1) * lanes
                        ]
        for to in (slot, opposite):
            copy = pltpu.make_async_copy(piece_ref.at[to], outs[to], sems.at[to])
            copy.start()
            copies.append(copy)
    for copy in copies:
        copy.wait()


def table_kernel(after_ref, out_ref):
    half = out_ref.shape[1]
    length = 2 * half
    width = half // 4
    rows = 64
    for distance in range(4):
        for at in range(0, width, rows):
            n = (
                lax.broadcasted_iota(jnp.int32, (rows, width), 0)
                - lax.broadcasted_iota(jnp.int32, (rows, width), 1)
                + (distance * width + at)
            )
            cosine, sine = cos_sin(n & (length - 1), length)
            factor = jnp.where((n & 1) == 1, 1.0 / length, -1.0 / length)
            inverse = jnp.where(n == 0, 0.0, factor / jnp.where(n == 0, 1.0, sine))
            parts = split_two(cosine * inverse) + split_two(inverse)
            for column in range(4):
                row = (column + distance) % 4
                for i, part in enumerate(parts):
                    wrapped = i >= 2 and row < column
                    out_ref[
                        i,
                        row * width + at : row * width + at + rows,
                        column * width : (column + 1) * width,
                    ] = -part if wrapped else part


def circulant_kernel(pair, place_ref, recv_ref, table_ref, turn_ref, near_ref, far_ref):
    group = place_ref[1] ^ pair
    half = recv_ref.shape[0] // 2
    top, bottom = recv_ref[:half, :], recv_ref[half:, :]
    turn = turn_ref[...]

    def operands(x):
        return [dot(part, turn).astype(bf16) for part in split_two(x)]

    plus, minus = operands(top + bottom), operands(top - bottom)
    count = half // 2
    first = pl.multiple_of((group & 1) * count, count)
    swapped = group >= 2
    rows = 256
    for at in range(0, count, rows):
        here = pl.ds(first + at, rows)

        def product(which, high, low):
            return dot(table_ref[2 * which, here, :], high) + (
                dot(table_ref[2 * which, here, :], low) + dot(table_ref[2 * which + 1, here, :], high)
            )

        even, odd = product(0, *plus), product(1, *minus)
        near_ref[at : at + rows, :] = even + jnp.where(swapped, -odd, odd)
        far_ref[at : at + rows, :] = even + jnp.where(swapped, odd, -odd)


def final_kernel(sizes, place_ref, mask_ref, *refs):
    planes, rows, slab, pens = sizes
    firsts, seconds, out_hbm = refs[:pens], refs[pens : pens + 4], refs[pens + 4]
    first_ref, second_ref, piece_ref, sems = refs[pens + 5 :]
    lanes = 128
    tiles = slab // lanes
    step = 2 * planes * tiles
    loads = [
        pltpu.make_async_copy(ref, second_ref.at[k], sems.at[2 * pens + k])
        for k, ref in enumerate(seconds)
    ] + [
        pltpu.make_async_copy(ref, first_ref.at[k], sems.at[k]) for k, ref in enumerate(firsts)
    ]
    for load in loads:
        load.start()
    pen, group = place_ref[0], place_ref[1]
    upper = pen >= pens // 2
    low_bit, high_bit = (group & 1) == 1, group >= 2
    special = mask_ref[...] > 0.0
    for load in loads[:4]:
        load.wait()
    stores = []
    for slot in range(pens):
        source = pen ^ slot
        here = pl.ds(pl.multiple_of(source * rows, rows), rows)
        r = [second_ref[k, here, :] for k in range(4)]
        r = [jnp.where(low_bit, r[k ^ 1], r[k]) for k in range(4)]
        r = [jnp.where(high_bit, r[k ^ 2], r[k]) for k in range(4)]
        loads[4 + slot].wait()
        for plane in range(planes):
            s, c = r[plane], r[planes + plane]
            pieces = (
                jnp.where(special, 0.0, jnp.where(upper, s, -s)),
                jnp.where(special & upper, -s, -c),
            )
            for part in range(2):
                for tile in range(tiles):
                    there = pl.ds((part * tiles + tile) * planes + plane, rows, stride=step)
                    piece_ref[slot, there, :] = (
                        first_ref[slot, there, :]
                        + pieces[part][:, tile * lanes : (tile + 1) * lanes]
                    )
        size = rows * step
        store = pltpu.make_async_copy(
            piece_ref.at[slot],
            out_hbm.at[pl.ds(pl.multiple_of(source * size, size), size)],
            sems.at[pens + slot],
        )
        store.start()
        stores.append(store)
    for store in stores:
        store.wait()


SPACES = {"s": pltpu.SMEM, "v": pltpu.VMEM, "h": pltpu.HBM, "a": pl.ANY}


def kernel_call(body, shapes, spaces, flops, moved, limit, scratch=()):
    inputs, outputs = spaces.split(">")
    specs = [pl.BlockSpec(memory_space=SPACES[s]) for s in outputs]
    return pl.pallas_call(
        body,
        out_shape=shapes,
        in_specs=[pl.BlockSpec(memory_space=SPACES[s]) for s in inputs],
        out_specs=specs if isinstance(shapes, list) else specs[0],
        scratch_shapes=scratch,
        cost_estimate=pl.CostEstimate(flops=flops, bytes_accessed=moved, transcendentals=0),
        compiler_params=pltpu.CompilerParams(vmem_limit_bytes=limit * 2**20),
    )


def exchange(block, axis, distance):
    size = lax.axis_size(axis)
    return lax.ppermute(block, axis, [(i, i ^ distance) for i in range(size)])


def fast_path(u, v, ky_order, sizes, groups):
    planes, rows, slab, pens = sizes
    length_y = v.shape[1]
    group_rows = rows * pens
    length_z = group_rows * groups
    half = length_y // 2
    lanes = 128
    pen, group = lax.axis_index("pen"), lax.axis_index("grp")
    place = jnp.stack([pen, group]).astype(jnp.int32)
    order = ky_order[None, :]
    flops = 2 * 3 * planes * rows * length_y * length_y
    dma = pltpu.SemaphoreType.DMA
    field = pltpu.VMEM(v.shape, f32)
    table = pltpu.VMEM((2, length_y // 4, length_y), bf16)
    v_blocks = kernel_call(
        functools.partial(second_kernel, sizes),
        jax.ShapeDtypeStruct((2 * planes, pens, rows, slab), f32),
        "vh>h",
        flops,
        2**22,
        60,
        [field, table, pltpu.VMEM((pens // 2, 2 * planes, rows, slab), f32), dma((pens + 1,))],
    )(order, v)
    recv = lax.all_to_all(
        v_blocks.reshape(groups * pens, rows, slab), ("grp", "pen"), 0, 0, tiled=True
    ).reshape(length_z, slab)
    swap = jnp.asarray(np.eye(slab)[::-1].copy(), bf16)
    size = rows * 2 * planes * slab // lanes
    firsts = kernel_call(
        functools.partial(first_kernel, sizes),
        [jax.ShapeDtypeStruct((size, lanes), f32)] * pens,
        "svvh>" + "h" * pens,
        flops,
        2**22,
        60,
        [field, table, pltpu.VMEM((pens, size, lanes), f32), dma((pens + 1,))],
    )(place, order, swap, u)
    circulant = kernel_call(
        table_kernel,
        jax.ShapeDtypeStruct((4, length_z // 2, length_z // 2), bf16),
        "a>v",
        2**24,
        2**23,
        16,
    )(firsts[0])
    arrived = {0: firsts[0]}
    for k in reversed(range(1, pens)):
        arrived[k] = exchange(firsts[k], "pen", k)
    turn = jnp.where(pen >= pens // 2, swap, jnp.asarray(np.eye(slab), bf16))
    seconds = [None] * groups
    for pair in range(2):
        both = kernel_call(
            functools.partial(circulant_kernel, pair),
            [jax.ShapeDtypeStruct((group_rows, slab), f32)] * 2,
            "svvv>vv",
            3 * length_z * length_z * slab // 2,
            2**23,
            20,
        )(place, recv, circulant, turn)
        for k, values in zip((pair, pair + 2), both):
            seconds[k] = exchange(values, "grp", k) if k else values
    mine = lax.dynamic_slice_in_dim(ky_order, pen * slab, slab)
    special = ((mine == 0) | (mine == half)).astype(f32)[None, :]
    result = kernel_call(
        functools.partial(final_kernel, sizes),
        jax.ShapeDtypeStruct((pens * size, lanes), f32),
        "sv" + "a" * (pens + groups) + ">h",
        2**23,
        2**22,
        16,
        [
            pltpu.VMEM((pens, size, lanes), f32),
            pltpu.VMEM((groups, group_rows, slab), f32),
            pltpu.VMEM((pens, size, lanes), f32),
            dma((2 * pens + groups,)),
        ],
    )(place, special, *[arrived[k] for k in range(pens)], *seconds)
    result = result.reshape(group_rows, 2, slab // lanes, planes, lanes)
    return jnp.transpose(result, (0, 1, 3, 2, 4)).reshape(group_rows, 2, planes, slab)


def whole_tables(length):
    half = length // 2
    n = lax.broadcasted_iota(jnp.int32, (half, half), 0) - lax.broadcasted_iota(
        jnp.int32, (half, half), 1
    )
    theta = 2.0 * math.pi / length * n.astype(f32)
    factor = jnp.where(n % 2 == 0, -1.0 / length, 1.0 / length)
    inverse = jnp.where(n == 0, 0.0, factor / jnp.where(n == 0, 1.0, jnp.sin(theta)))
    return jnp.cos(theta) * inverse, inverse


def plain_path(u, v, ky_order, sizes, groups):
    planes, rows, slab, pens = sizes
    length_y = v.shape[1]
    group_rows = rows * pens
    length_z = group_rows * groups
    half = length_y // 2
    exact = lax.Precision.HIGHEST
    pen = lax.axis_index("pen")
    upper = pen >= pens // 2
    waves = ky_order[:half]
    index = lax.iota(jnp.int32, length_y)[:, None]
    theta = 2.0 * math.pi / length_y * (index * waves[None, :] % length_y).astype(f32)
    mixed = 2.0 * math.pi / length_y * (index * (half - waves[None, :]) % length_y).astype(f32)
    special = (waves == 0) | (waves == half)
    sines = jnp.where(special, jnp.cos(mixed), jnp.sin(theta))
    both = 1.0 / math.sqrt(length_y) * jnp.stack([sines, jnp.cos(theta)])

    def transform(x):
        y = jnp.einsum("ry,pyk->prk", x, both, precision=exact)
        return y.reshape(2, planes, rows, pens // 2, slab)

    y = transform(v)
    y = jnp.concatenate([y, jnp.flip(y, 3)], 3)
    v_blocks = jnp.transpose(y, (3, 2, 0, 1, 4)).reshape(pens, rows, groups, -1)
    v_blocks = jnp.transpose(v_blocks, (2, 0, 1, 3)).reshape(groups * pens, rows, -1)
    y = transform(u) * signed_scale(waves, length_y).reshape(pens // 2, slab)
    turned = jnp.flip(y, (3, 4)) * jnp.array([1.0, -1.0], f32)[:, None, None, None, None]
    u_blocks = jnp.transpose(jnp.concatenate([y, turned], 3), (3, 2, 0, 1, 4))
    recv = lax.all_to_all(v_blocks, ("grp", "pen"), 0, 0, tiled=True).reshape(length_z, -1)
    u_recv = lax.all_to_all(u_blocks, "pen", 0, 0, tiled=True)
    table = whole_tables(length_z)
    top, bottom = recv[: length_z // 2], recv[length_z // 2 :]
    even = jnp.dot(table[0], top + bottom, precision=exact)
    odd = jnp.dot(table[1], top - bottom, precision=exact)
    deriv = jnp.concatenate([even + odd, even - odd], 0)
    back = lax.all_to_all(deriv.reshape(groups, group_rows, -1), "grp", 0, 0, tiled=True)
    back = jnp.transpose(back, (1, 0, 2)).reshape(group_rows, 2, planes, slab)
    back = jnp.where(upper, jnp.flip(back, 3), back)
    mine = lax.dynamic_slice_in_dim(ky_order, pen * slab, slab)
    special = (mine == 0) | (mine == half)
    s, c = back[:, 0], back[:, 1]
    first = jnp.where(special, 0.0, jnp.where(upper, s, -s))
    second = jnp.where(special & upper, -s, -c)
    return u_recv.reshape(group_rows, 2, planes, slab) + jnp.stack([first, second], 1)


def on_device(u_field, v_field, ky_order):
    planes, rows, length_y = u_field.shape
    pens, groups = lax.axis_size("pen"), lax.axis_size("grp")
    slab = length_y // pens
    u = u_field.reshape(planes * rows, length_y)
    v = v_field.reshape(planes * rows, length_y)
    fast = slab % 128 == 0 and rows % 8 == 0 and groups == 4 and planes == 2 and pens % 4 == 0
    fast = fast and length_y % 1024 == 0 and length_y & (length_y - 1) == 0 and pens & (pens - 1) == 0
    path = fast_path if fast else plain_path
    return path(u, v, ky_order, (planes, rows, slab, pens), groups)


def solution(mesh):
    placed = (P(None, ("grp", "pen"), None), P(None, ("grp", "pen"), None), P())

    return jax.shard_map(
        on_device,
        mesh=mesh,
        in_specs=placed,
        out_specs=P("grp", None, None, "pen"),
        check_vma=False,
    )
```

```python
import functools
import math

import jax
import jax.numpy as jnp
import numpy as np
from jax import lax
from jax.experimental import pallas as pl
from jax.experimental.pallas import tpu as pltpu
from jax.sharding import PartitionSpec as P


f32 = jnp.float32
bf16 = jnp.bfloat16


def split_two(x):
    high = x.astype(bf16)
    return high, (x - high.astype(f32)).astype(bf16)


def split_three(x):
    high = x.astype(bf16)
    rest = x - high.astype(f32)
    middle = rest.astype(bf16)
    return high, middle, (rest - middle.astype(f32)).astype(bf16)


def dot(a, b):
    return jnp.dot(a, b, preferred_element_type=f32)


def signed_scale(waves, length):
    signed = jnp.where(waves < length // 2, waves, waves - length)
    signed = jnp.where(waves == length // 2, 0, signed)
    return 2.0 / length * signed.astype(f32)


def cos_sin(residue, length):
    eighth = length // 8
    turned = (residue + eighth) & (length - 1)
    turn = turned // (2 * eighth)
    x = (2.0 * math.pi / length) * (turned - turn * (2 * eighth) - eighth).astype(f32)
    y = x * x
    cosine = 1.0 + y * (-1 / 2 + y * (1 / 24 + y * (-1 / 720 + y * (1 / 40320))))
    sine = x * (1.0 + y * (-1 / 6 + y * (1 / 120 + y * (-1 / 5040 + y * (1 / 362880)))))
    odd = (turn & 1) == 1
    first, second = jnp.where(odd, sine, cosine), jnp.where(odd, cosine, sine)
    return (
        jnp.where((turn == 1) | (turn == 2), -first, first),
        jnp.where(turn >= 2, -second, second),
    )


def reverse_lanes(x, swap):
    high, middle, low = split_three(x)
    return dot(high, swap) + (dot(middle, swap) + dot(low, swap))


def transform_block(fields, table_ref, waves, first, slab):
    field_high, field_low = fields
    rows = field_high.shape[0] // 4
    half = table_ref.shape[2] // 2
    sums = []
    for part in range(2):
        columns = pl.ds(part * half + first, slab)
        high, low = table_ref[0, :, columns], table_ref[1, :, columns]
        sums.append(dot(field_high, high) + (dot(field_high, low) + dot(field_low, high)))
    residue = waves & 3
    sign = jnp.where((residue & 1) == 1, -1.0, 1.0)
    cosine = jnp.where(residue == 0, 1.0, jnp.where(residue == 2, -1.0, 0.0))
    sine = jnp.where(residue == 1, 1.0, jnp.where(residue == 3, -1.0, 0.0))

    def folded(x):
        return (
            x[:rows] + sign * x[2 * rows : 3 * rows],
            x[rows : 2 * rows] + sign * x[3 * rows :],
        )

    even_c, odd_c = folded(sums[0])
    even_s, odd_s = folded(sums[1])
    return (
        even_c + cosine * odd_c - sine * odd_s,
        even_s + cosine * odd_s + sine * odd_c,
    )


def fill_table(waves, table_ref, length):
    half = waves.shape[1]
    norm = 1.0 / math.sqrt(length)
    fine = 32
    coarse = length // 4 // fine
    special = (waves == 0) | (waves == length // 2)
    coarse_c, coarse_s = cos_sin(
        (fine * lax.broadcasted_iota(jnp.int32, (coarse, half), 0) * waves) & (length - 1), length
    )
    coarse_c, coarse_s = norm * coarse_c, norm * coarse_s
    index = lax.broadcasted_iota(jnp.int32, (fine, half), 0)
    fine_c, fine_s = cos_sin((index * waves) & (length - 1), length)
    other = norm * jnp.where((waves == 0) & ((index & 1) == 1), -1.0, 1.0)
    for a in range(coarse):
        this_c, this_s = coarse_c[a : a + 1], coarse_s[a : a + 1]
        here = slice(a * fine, (a + 1) * fine)
        cosines = this_c * fine_c - this_s * fine_s
        sines = this_c * fine_s + this_s * fine_c
        sines = jnp.where(special, other, sines)
        for part, values in enumerate((cosines, sines)):
            high, low = split_two(values)
            table_ref[0, here, part * half : (part + 1) * half] = high
            table_ref[1, here, part * half : (part + 1) * half] = low


def load_quarters(ref):
    quarter = ref.shape[1] // 4
    x = jnp.concatenate([ref[:, i * quarter : (i + 1) * quarter] for i in range(4)], 0)
    return split_two(x)


def second_kernel(sizes, tile, order_ref, field_hbm, out_hbm, field_ref, table_ref, piece_ref, sems):
    planes, rows, slab, pens = sizes
    lanes = 128
    load = pltpu.make_async_copy(field_hbm, field_ref, sems.at[pens])
    load.start()
    starts = [block * slab + tile * lanes for block in range(pens // 2)]
    waves = jnp.concatenate([order_ref[:, at : at + lanes] for at in starts], 1)
    fill_table(waves, table_ref, order_ref.shape[1])
    load.wait()
    fields = load_quarters(field_ref)
    copies = []
    for pair in range(pens // 4):
        first = 2 * pair * lanes
        here = waves[:, first : first + 2 * lanes]
        c, s = transform_block(fields, table_ref, here, first, 2 * lanes)
        for side in range(2):
            block = 2 * pair + side
            columns = slice(side * lanes, (side + 1) * lanes)
            for part, values in enumerate((s, c)):
                for plane in range(planes):
                    piece_ref[block, part * planes + plane] = values[
                        plane * rows : (plane + 1) * rows, columns
                    ]
            for target in (block, pens - 1 - block):
                copy = pltpu.make_async_copy(
                    piece_ref.at[block], out_hbm.at[:, target], sems.at[target]
                )
                copy.start()
                copies.append(copy)
    for copy in copies:
        copy.wait()


def first_kernel(sizes, place_ref, order_ref, swap_ref, field_hbm, *refs):
    planes, rows, slab, pens = sizes
    outs, (field_ref, table_ref, piece_ref, sems) = refs[:pens], refs[pens:]
    load = pltpu.make_async_copy(field_hbm, field_ref, sems.at[pens])
    load.start()
    length = order_ref.shape[1]
    fill_table(order_ref[:, : length // 2], table_ref, length)
    load.wait()
    fields = load_quarters(field_ref)
    pen = place_ref[0]
    upper = pen >= pens // 2
    lanes = 128
    step = 2 * planes * (slab // lanes)
    copies = []
    for slot in range(pens // 2):
        target = pen ^ slot
        block = jnp.where(upper, pens - 1 - target, target)
        first = pl.multiple_of(block * slab, slab)
        waves = order_ref[:, pl.ds(first, slab)]
        c, s = transform_block(fields, table_ref, waves, first, slab)
        scale = signed_scale(waves, length)
        opposite = slot ^ (pens - 1)
        for part, values in enumerate((scale * s, scale * c)):
            turned = reverse_lanes(values, swap_ref[...])
            if part == 1:
                turned = -turned
            near, far = jnp.where(upper, turned, values), jnp.where(upper, values, turned)
            for to, piece in ((slot, near), (opposite, far)):
                for plane in range(planes):
                    for tile in range(slab // lanes):
                        at = (part * (slab // lanes) + tile) * planes + plane
                        piece_ref[to, pl.ds(at, rows, stride=step), :] = piece[
                            plane * rows : (plane + 1) * rows, tile * lanes : (tile + 1) * lanes
                        ]
        for to in (slot, opposite):
            copy = pltpu.make_async_copy(piece_ref.at[to], outs[to], sems.at[to])
            copy.start()
            copies.append(copy)
    for copy in copies:
        copy.wait()


def table_kernel(after_ref, out_ref):
    width = out_ref.shape[2]
    length = 8 * width
    rows = 64
    for distance in range(4):
        for at in range(0, width, rows):
            n = (
                lax.broadcasted_iota(jnp.int32, (rows, width), 0)
                - lax.broadcasted_iota(jnp.int32, (rows, width), 1)
                + (distance * width + at)
            )
            cosine, sine = cos_sin(n & (length - 1), length)
            factor = jnp.where((n & 1) == 1, 1.0 / length, -1.0 / length)
            inverse = jnp.where(n == 0, 0.0, factor / jnp.where(n == 0, 1.0, sine))
            here = slice(at, at + rows)
            for i, part in enumerate(split_two(cosine * inverse)):
                out_ref[i, distance, here, :] = part
            for i, part in enumerate(split_two(inverse)):
                out_ref[i, 4 + distance, here, :] = part
                if distance:
                    out_ref[i, 7 + distance, here, :] = -part


def circulant_kernel(place_ref, recv_ref, table_ref, turn_ref, *out_refs):
    half = recv_ref.shape[0] // 2
    lanes = recv_ref.shape[1]
    width = half // 4
    top, bottom = recv_ref[:half, :], recv_ref[half:, :]
    turn = turn_ref[...]

    def operand(x):
        return dot(jnp.concatenate(split_two(x), 1), turn).astype(bf16)

    plus, minus = operand(top + bottom), operand(top - bottom)
    for pair in range(2):
        group = place_ref[1] ^ pair
        swapped = group >= 2
        for i in range(2):
            row = 2 * (group & 1) + i

            def product(x, index):
                high, low = [
                    jnp.concatenate([table_ref[w, index(column)] for column in range(4)], 1)
                    for w in range(2)
                ]
                both = dot(high, x)
                return both[:, :lanes] + (both[:, lanes:] + dot(low, x[:, :lanes]))

            even = product(plus, lambda column: (row - column) & 3)
            odd = product(
                minus, lambda column: row - column + jnp.where(row >= column, 4, 11)
            )
            here = slice(i * width, (i + 1) * width)
            out_refs[pair][here, :] = even + jnp.where(swapped, -odd, odd)
            out_refs[pair + 2][here, :] = even + jnp.where(swapped, odd, -odd)


def final_kernel(sizes, place_ref, mask_ref, *refs):
    planes, rows, slab, pens = sizes
    lanes = 128
    tiles = slab // lanes
    step = 2 * planes * tiles
    count = 4 * tiles
    firsts, seconds, out_hbm = refs[:pens], refs[pens : pens + count], refs[pens + count]
    first_ref, second_ref, piece_ref, sems = refs[pens + count + 1 :]
    loads = [
        pltpu.make_async_copy(ref, second_ref.at[k], sems.at[2 * pens + k])
        for k, ref in enumerate(seconds)
    ] + [
        pltpu.make_async_copy(ref, first_ref.at[k], sems.at[k]) for k, ref in enumerate(firsts)
    ]
    for load in loads:
        load.start()
    pen, group = place_ref[0], place_ref[1]
    upper = pen >= pens // 2
    for load in loads[:count]:
        load.wait()
    stores = []
    for slot in range(pens):
        source = pen ^ slot
        here = pl.ds(pl.multiple_of(source * rows, rows), rows)
        loads[count + slot].wait()
        for tile in range(tiles):
            special = mask_ref[:, tile * lanes : (tile + 1) * lanes] > 0.0
            base = 4 * jnp.where(upper, tiles - 1 - tile, tile)
            for plane in range(planes):
                s = second_ref[base + (plane ^ group), here, :]
                c = second_ref[base + ((planes + plane) ^ group), here, :]
                pieces = (
                    jnp.where(special, 0.0, jnp.where(upper, s, -s)),
                    jnp.where(special & upper, -s, -c),
                )
                for part in range(2):
                    there = pl.ds((part * tiles + tile) * planes + plane, rows, stride=step)
                    piece_ref[slot, there, :] = first_ref[slot, there, :] + pieces[part]
        size = rows * step
        store = pltpu.make_async_copy(
            piece_ref.at[slot],
            out_hbm.at[pl.ds(pl.multiple_of(source * size, size), size)],
            sems.at[pens + slot],
        )
        store.start()
        stores.append(store)
    for store in stores:
        store.wait()


SPACES = {"s": pltpu.SMEM, "v": pltpu.VMEM, "h": pltpu.HBM, "a": pl.ANY}


def kernel_call(body, shapes, spaces, flops, moved, limit, scratch=()):
    inputs, outputs = spaces.split(">")
    specs = [pl.BlockSpec(memory_space=SPACES[s]) for s in outputs]
    return pl.pallas_call(
        body,
        out_shape=shapes,
        in_specs=[pl.BlockSpec(memory_space=SPACES[s]) for s in inputs],
        out_specs=specs if isinstance(shapes, list) else specs[0],
        scratch_shapes=scratch,
        cost_estimate=pl.CostEstimate(flops=flops, bytes_accessed=moved, transcendentals=0),
        compiler_params=pltpu.CompilerParams(vmem_limit_bytes=limit * 2**20),
    )


def exchange(block, axis, distance):
    size = lax.axis_size(axis)
    return lax.ppermute(block, axis, [(i, i ^ distance) for i in range(size)])


def fast_path(u, v, ky_order, sizes, groups):
    planes, rows, slab, pens = sizes
    length_y = v.shape[1]
    group_rows = rows * pens
    length_z = group_rows * groups
    half = length_y // 2
    lanes = 128
    pen, group = lax.axis_index("pen"), lax.axis_index("grp")
    place = jnp.stack([pen, group]).astype(jnp.int32)
    order = ky_order[None, :]
    flops = 2 * 3 * planes * rows * length_y * length_y
    dma = pltpu.SemaphoreType.DMA
    field = pltpu.VMEM(v.shape, f32)
    table = pltpu.VMEM((2, length_y // 4, length_y), bf16)
    tiles = slab // lanes
    recv = []
    for tile in range(tiles):
        v_blocks = kernel_call(
            functools.partial(second_kernel, sizes, tile),
            jax.ShapeDtypeStruct((2 * planes, pens, rows, lanes), f32),
            "vh>h",
            flops // tiles,
            2**21,
            60,
            [
                field,
                pltpu.VMEM((2, length_y // 4, length_y // tiles), bf16),
                pltpu.VMEM((pens // 2, 2 * planes, rows, lanes), f32),
                dma((pens + 1,)),
            ],
        )(order, v)
        v_blocks = v_blocks.reshape(groups * pens, rows, lanes)
        v_blocks = lax.all_to_all(v_blocks, ("grp", "pen"), 0, 0, tiled=True)
        recv.append(v_blocks.reshape(length_z, lanes))
    swap = jnp.asarray(np.eye(slab)[::-1].copy(), bf16)
    size = rows * 2 * planes * slab // lanes
    firsts = kernel_call(
        functools.partial(first_kernel, sizes),
        [jax.ShapeDtypeStruct((size, lanes), f32)] * pens,
        "svvh>" + "h" * pens,
        flops,
        2**22,
        60,
        [field, table, pltpu.VMEM((pens, size, lanes), f32), dma((pens + 1,))],
    )(place, order, swap, u)
    circulant = kernel_call(
        table_kernel,
        jax.ShapeDtypeStruct((2, 11, length_z // 8, length_z // 8), bf16),
        "a>v",
        2**24,
        2**21,
        16,
    )(firsts[0])
    arrived = {0: firsts[0]}
    for k in reversed(range(1, pens)):
        arrived[k] = exchange(firsts[k], "pen", k)
    flip = np.kron(np.eye(2), np.eye(lanes)[::-1])
    turn = jnp.where(pen >= pens // 2, jnp.asarray(flip, bf16), jnp.asarray(np.eye(2 * lanes), bf16))
    seconds = []
    for tile in range(tiles):
        parts = kernel_call(
            circulant_kernel,
            [jax.ShapeDtypeStruct((group_rows, lanes), f32)] * groups,
            "svvv>vvvv",
            3 * length_z * length_z * lanes,
            2**22,
            20,
        )(place, recv[tile], circulant, turn)
        seconds.append(parts[0])
        for k in range(1, groups):
            seconds.append(exchange(parts[k], "grp", k))
    mine = lax.dynamic_slice_in_dim(ky_order, pen * slab, slab)
    special = ((mine == 0) | (mine == half)).astype(f32)[None, :]
    result = kernel_call(
        functools.partial(final_kernel, sizes),
        jax.ShapeDtypeStruct((pens * size, lanes), f32),
        "sv" + "a" * (pens + groups * tiles) + ">h",
        2**23,
        2**22,
        16,
        [
            pltpu.VMEM((pens, size, lanes), f32),
            pltpu.VMEM((groups * tiles, group_rows, lanes), f32),
            pltpu.VMEM((pens, size, lanes), f32),
            dma((2 * pens + groups * tiles,)),
        ],
    )(place, special, *[arrived[k] for k in range(pens)], *seconds)
    result = result.reshape(group_rows, 2, tiles, planes, lanes)
    return jnp.transpose(result, (0, 1, 3, 2, 4)).reshape(group_rows, 2, planes, slab)


def whole_tables(length):
    half = length // 2
    n = lax.broadcasted_iota(jnp.int32, (half, half), 0) - lax.broadcasted_iota(
        jnp.int32, (half, half), 1
    )
    theta = 2.0 * math.pi / length * n.astype(f32)
    factor = jnp.where(n % 2 == 0, -1.0 / length, 1.0 / length)
    inverse = jnp.where(n == 0, 0.0, factor / jnp.where(n == 0, 1.0, jnp.sin(theta)))
    return jnp.cos(theta) * inverse, inverse


def plain_path(u, v, ky_order, sizes, groups):
    planes, rows, slab, pens = sizes
    length_y = v.shape[1]
    group_rows = rows * pens
    length_z = group_rows * groups
    half = length_y // 2
    exact = lax.Precision.HIGHEST
    pen = lax.axis_index("pen")
    upper = pen >= pens // 2
    waves = ky_order[:half]
    index = lax.iota(jnp.int32, length_y)[:, None]
    theta = 2.0 * math.pi / length_y * (index * waves[None, :] % length_y).astype(f32)
    mixed = 2.0 * math.pi / length_y * (index * (half - waves[None, :]) % length_y).astype(f32)
    special = (waves == 0) | (waves == half)
    sines = jnp.where(special, jnp.cos(mixed), jnp.sin(theta))
    both = 1.0 / math.sqrt(length_y) * jnp.stack([sines, jnp.cos(theta)])

    def transform(x):
        y = jnp.einsum("ry,pyk->prk", x, both, precision=exact)
        return y.reshape(2, planes, rows, pens // 2, slab)

    y = transform(v)
    y = jnp.concatenate([y, jnp.flip(y, 3)], 3)
    v_blocks = jnp.transpose(y, (3, 2, 0, 1, 4)).reshape(pens, rows, groups, -1)
    v_blocks = jnp.transpose(v_blocks, (2, 0, 1, 3)).reshape(groups * pens, rows, -1)
    y = transform(u) * signed_scale(waves, length_y).reshape(pens // 2, slab)
    turned = jnp.flip(y, (3, 4)) * jnp.array([1.0, -1.0], f32)[:, None, None, None, None]
    u_blocks = jnp.transpose(jnp.concatenate([y, turned], 3), (3, 2, 0, 1, 4))
    recv = lax.all_to_all(v_blocks, ("grp", "pen"), 0, 0, tiled=True).reshape(length_z, -1)
    u_recv = lax.all_to_all(u_blocks, "pen", 0, 0, tiled=True)
    table = whole_tables(length_z)
    top, bottom = recv[: length_z // 2], recv[length_z // 2 :]
    even = jnp.dot(table[0], top + bottom, precision=exact)
    odd = jnp.dot(table[1], top - bottom, precision=exact)
    deriv = jnp.concatenate([even + odd, even - odd], 0)
    back = lax.all_to_all(deriv.reshape(groups, group_rows, -1), "grp", 0, 0, tiled=True)
    back = jnp.transpose(back, (1, 0, 2)).reshape(group_rows, 2, planes, slab)
    back = jnp.where(upper, jnp.flip(back, 3), back)
    mine = lax.dynamic_slice_in_dim(ky_order, pen * slab, slab)
    special = (mine == 0) | (mine == half)
    s, c = back[:, 0], back[:, 1]
    first = jnp.where(special, 0.0, jnp.where(upper, s, -s))
    second = jnp.where(special & upper, -s, -c)
    return u_recv.reshape(group_rows, 2, planes, slab) + jnp.stack([first, second], 1)


def on_device(u_field, v_field, ky_order):
    planes, rows, length_y = u_field.shape
    pens, groups = lax.axis_size("pen"), lax.axis_size("grp")
    slab = length_y // pens
    u = u_field.reshape(planes * rows, length_y)
    v = v_field.reshape(planes * rows, length_y)
    fast = slab % 128 == 0 and rows % 8 == 0 and groups == 4 and planes == 2 and pens % 4 == 0
    fast = fast and length_y % 1024 == 0 and length_y & (length_y - 1) == 0 and pens & (pens - 1) == 0
    path = fast_path if fast else plain_path
    return path(u, v, ky_order, (planes, rows, slab, pens), groups)


def solution(mesh):
    placed = (P(None, ("grp", "pen"), None), P(None, ("grp", "pen"), None), P())

    return jax.shard_map(
        on_device,
        mesh=mesh,
        in_specs=placed,
        out_specs=P("grp", None, None, "pen"),
        check_vma=False,
    )
```

```python
import functools
import math

import jax
import jax.numpy as jnp
import numpy as np
from jax import lax
from jax.experimental import pallas as pl
from jax.experimental.pallas import tpu as pltpu
from jax.sharding import PartitionSpec as P


LAST = (5, 6)
SLOTS = (0, 1, 2, 3)
f32 = jnp.float32
bf16 = jnp.bfloat16


def split_two(x):
    high = x.astype(bf16)
    return high, (x - high.astype(f32)).astype(bf16)


def split_three(x):
    high = x.astype(bf16)
    rest = x - high.astype(f32)
    middle = rest.astype(bf16)
    return high, middle, (rest - middle.astype(f32)).astype(bf16)


def dot(a, b):
    return jnp.dot(a, b, preferred_element_type=f32)


def signed_scale(waves, length):
    signed = jnp.where(waves < length // 2, waves, waves - length)
    signed = jnp.where(waves == length // 2, 0, signed)
    return 2.0 / length * signed.astype(f32)


def cos_sin(residue, length):
    eighth = length // 8
    turned = (residue + eighth) & (length - 1)
    turn = turned // (2 * eighth)
    x = (2.0 * math.pi / length) * (turned - turn * (2 * eighth) - eighth).astype(f32)
    y = x * x
    cosine = 1.0 + y * (-1 / 2 + y * (1 / 24 + y * (-1 / 720 + y * (1 / 40320))))
    sine = x * (1.0 + y * (-1 / 6 + y * (1 / 120 + y * (-1 / 5040 + y * (1 / 362880)))))
    odd = (turn & 1) == 1
    first, second = jnp.where(odd, sine, cosine), jnp.where(odd, cosine, sine)
    return (
        jnp.where((turn == 1) | (turn == 2), -first, first),
        jnp.where(turn >= 2, -second, second),
    )


def reverse_lanes(x, swap):
    high, middle, low = split_three(x)
    return dot(high, swap) + (dot(middle, swap) + dot(low, swap))


def transform_block(fields, table_ref, waves, first, slab):
    field_high, field_low = fields
    rows = field_high.shape[0] // 4
    half = table_ref.shape[2] // 2
    sums = []
    for part in range(2):
        columns = pl.ds(part * half + first, slab)
        high, low = table_ref[0, :, columns], table_ref[1, :, columns]
        sums.append(dot(field_high, high) + (dot(field_high, low) + dot(field_low, high)))
    residue = waves & 3
    sign = jnp.where((residue & 1) == 1, -1.0, 1.0)
    cosine = jnp.where(residue == 0, 1.0, jnp.where(residue == 2, -1.0, 0.0))
    sine = jnp.where(residue == 1, 1.0, jnp.where(residue == 3, -1.0, 0.0))

    def folded(x):
        return (
            x[:rows] + sign * x[2 * rows : 3 * rows],
            x[rows : 2 * rows] + sign * x[3 * rows :],
        )

    even_c, odd_c = folded(sums[0])
    even_s, odd_s = folded(sums[1])
    return (
        even_c + cosine * odd_c - sine * odd_s,
        even_s + cosine * odd_s + sine * odd_c,
    )


def fill_table(waves, table_ref, length):
    half = waves.shape[1]
    norm = 1.0 / math.sqrt(length)
    fine = 32
    coarse = length // 4 // fine
    special = (waves == 0) | (waves == length // 2)
    coarse_c, coarse_s = cos_sin(
        (fine * lax.broadcasted_iota(jnp.int32, (coarse, half), 0) * waves) & (length - 1), length
    )
    coarse_c, coarse_s = norm * coarse_c, norm * coarse_s
    index = lax.broadcasted_iota(jnp.int32, (fine, half), 0)
    fine_c, fine_s = cos_sin((index * waves) & (length - 1), length)
    other = norm * jnp.where((waves == 0) & ((index & 1) == 1), -1.0, 1.0)
    for a in range(coarse):
        this_c, this_s = coarse_c[a : a + 1], coarse_s[a : a + 1]
        here = slice(a * fine, (a + 1) * fine)
        cosines = this_c * fine_c - this_s * fine_s
        sines = this_c * fine_s + this_s * fine_c
        sines = jnp.where(special, other, sines)
        for part, values in enumerate((cosines, sines)):
            high, low = split_two(values)
            table_ref[0, here, part * half : (part + 1) * half] = high
            table_ref[1, here, part * half : (part + 1) * half] = low


def load_quarters(ref):
    quarter = ref.shape[1] // 4
    x = jnp.concatenate([ref[:, i * quarter : (i + 1) * quarter] for i in range(4)], 0)
    return split_two(x)


def second_kernel(
    sizes, tile, order_hbm, field_hbm, out_hbm, order_ref, field_ref, table_ref, piece_ref, sems
):
    planes, rows, slab, pens = sizes
    lanes = 128
    first_load = pltpu.make_async_copy(order_hbm, order_ref, sems.at[pens + 1])
    first_load.start()
    load = pltpu.make_async_copy(field_hbm, field_ref, sems.at[pens])
    load.start()
    first_load.wait()
    starts = [block * slab + tile * lanes for block in range(pens // 2)]
    waves = jnp.concatenate([order_ref[:, at : at + lanes] for at in starts], 1)
    fill_table(waves, table_ref, order_ref.shape[1])
    load.wait()
    fields = load_quarters(field_ref)
    copies = []
    for pair in range(pens // 4):
        first = 2 * pair * lanes
        here = waves[:, first : first + 2 * lanes]
        c, s = transform_block(fields, table_ref, here, first, 2 * lanes)
        for side in range(2):
            block = 2 * pair + side
            columns = slice(side * lanes, (side + 1) * lanes)
            for part, values in enumerate((s, c)):
                for plane in range(planes):
                    piece_ref[block, part * planes + plane] = values[
                        plane * rows : (plane + 1) * rows, columns
                    ]
            for target in (block, pens - 1 - block):
                copy = pltpu.make_async_copy(
                    piece_ref.at[block], out_hbm.at[target], sems.at[target]
                )
                copy.start()
                copies.append(copy)
    for copy in copies:
        copy.wait()


def first_kernel(sizes, slots, place_ref, order_ref, swap_ref, field_hbm, *refs):
    planes, rows, slab, pens = sizes
    outs, (field_ref, table_ref, waves_ref, piece_ref, sems) = refs[:-5], refs[-5:]
    load = pltpu.make_async_copy(field_hbm, field_ref, sems.at[pens])
    load.start()
    length = order_ref.shape[1]
    pen = place_ref[0]
    upper = pen >= pens // 2
    for i, slot in enumerate(slots):
        target = pen ^ slot
        block = jnp.where(upper, pens - 1 - target, target)
        first = pl.multiple_of(block * slab, slab)
        waves_ref[:, i * slab : (i + 1) * slab] = order_ref[:, pl.ds(first, slab)]
    fill_table(waves_ref[...], table_ref, length)
    load.wait()
    fields = load_quarters(field_ref)
    lanes = 128
    step = 2 * planes * (slab // lanes)
    copies = []
    for i in range(len(slots)):
        waves = waves_ref[:, i * slab : (i + 1) * slab]
        c, s = transform_block(fields, table_ref, waves, i * slab, slab)
        scale = signed_scale(waves, length)
        for part, values in enumerate((scale * s, scale * c)):
            turned = reverse_lanes(values, swap_ref[...])
            if part == 1:
                turned = -turned
            near, far = jnp.where(upper, turned, values), jnp.where(upper, values, turned)
            for to, piece in ((2 * i, near), (2 * i + 1, far)):
                for plane in range(planes):
                    for tile in range(slab // lanes):
                        at = (part * (slab // lanes) + tile) * planes + plane
                        piece_ref[to, pl.ds(at, rows, stride=step), :] = piece[
                            plane * rows : (plane + 1) * rows, tile * lanes : (tile + 1) * lanes
                        ]
        for to in (2 * i, 2 * i + 1):
            copy = pltpu.make_async_copy(piece_ref.at[to], outs[to], sems.at[to])
            copy.start()
            copies.append(copy)
    for copy in copies:
        copy.wait()


def table_kernel(after_ref, out_ref):
    width = out_ref.shape[2]
    length = 8 * width
    rows = 64
    for distance in range(4):
        for at in range(0, width, rows):
            n = (
                lax.broadcasted_iota(jnp.int32, (rows, width), 0)
                - lax.broadcasted_iota(jnp.int32, (rows, width), 1)
                + (distance * width + at)
            )
            cosine, sine = cos_sin(n & (length - 1), length)
            factor = jnp.where((n & 1) == 1, 1.0 / length, -1.0 / length)
            inverse = jnp.where(n == 0, 0.0, factor / jnp.where(n == 0, 1.0, sine))
            here = slice(at, at + rows)
            for i, part in enumerate(split_two(cosine * inverse)):
                out_ref[i, distance, here, :] = part
            for i, part in enumerate(split_two(inverse)):
                out_ref[i, 4 + distance, here, :] = part
                if distance:
                    out_ref[i, 7 + distance, here, :] = -part


def circulant_kernel(place_ref, recv_ref, table_ref, turn_ref, *out_refs):
    count, rows, lanes = recv_ref.shape
    width = count * rows // 8
    turn = turn_ref[...]
    top, bottom = [
        jnp.concatenate(
            [recv_ref[4 * pen + group] for group in groups for pen in range(count // 4)], 0
        )
        for groups in ((0, 1), (2, 3))
    ]

    def operand(x):
        return dot(jnp.concatenate(split_two(x), 1), turn).astype(bf16)

    plus, minus = operand(top + bottom), operand(top - bottom)
    for pair in range(2):
        group = place_ref[1] ^ pair
        swapped = group >= 2
        for i in range(2):
            row = 2 * (group & 1) + i

            def product(x, index):
                both = jnp.concatenate(
                    [
                        jnp.concatenate([table_ref[w, index(column)] for column in range(4)], 1)
                        for w in range(2)
                    ],
                    0,
                )
                both = dot(both, x)
                return both[:width, :lanes] + (both[:width, lanes:] + both[width:, :lanes])

            even = product(plus, lambda column: (row - column) & 3)
            odd = product(
                minus, lambda column: row - column + jnp.where(row >= column, 4, 11)
            )
            here = slice(i * width, (i + 1) * width)
            out_refs[pair][here, :] = even + jnp.where(swapped, -odd, odd)
            out_refs[pair + 2][here, :] = even + jnp.where(swapped, odd, -odd)


def final_kernel(sizes, slots, place_ref, order_ref, *refs):
    planes, rows, slab, pens = sizes
    lanes = 128
    tiles = slab // lanes
    step = 2 * planes * tiles
    size = rows * step
    count = 4 * tiles
    firsts, seconds = refs[: len(slots)], refs[len(slots) : len(slots) + count]
    out_hbm, late_ref, piece_ref, sems = refs[-4:]
    pen, group = place_ref[0], place_ref[1]
    upper = pen >= pens // 2
    low_bit, high_bit = (group & 1) == 1, group >= 2
    waves = order_ref[:, pl.ds(pl.multiple_of(pen * slab, slab), slab)]
    specials = (waves == 0) | (waves == order_ref.shape[1] // 2)
    stores = []
    others = [slot for slot in range(1, pens) if slot not in slots]
    for at, slot in enumerate([*slots, *others]):
        source = pen ^ slot
        here = pl.ds(pl.multiple_of(source * rows, rows), rows)
        early = at < len(slots)
        r = [ref[here, :] for ref in seconds]
        r = [jnp.where(low_bit, r[k ^ 1], r[k]) for k in range(count)]
        r = [jnp.where(high_bit, r[k ^ 2], r[k]) for k in range(count)]
        if tiles == 2:
            r = [jnp.where(upper, r[k ^ 4], r[k]) for k in range(count)]
        for tile in range(tiles):
            special = specials[:, tile * lanes : (tile + 1) * lanes]
            base = 4 * tile
            for plane in range(planes):
                s, c = r[base + plane], r[base + planes + plane]
                pieces = (
                    jnp.where(special, 0.0, jnp.where(upper, s, -s)),
                    jnp.where(special & upper, -s, -c),
                )
                for part in range(2):
                    there = pl.ds((part * tiles + tile) * planes + plane, rows, stride=step)
                    if early:
                        piece_ref[at, there, :] = firsts[at][there, :] + pieces[part]
                    else:
                        late_ref[at - len(slots), there, :] = pieces[part]
        if early:
            store = pltpu.make_async_copy(
                piece_ref.at[at],
                out_hbm.at[pl.ds(pl.multiple_of(source * size, size), size)],
                sems.at[at],
            )
            store.start()
            stores.append(store)
    for store in stores:
        store.wait()


def last_kernel(slots, place_ref, late_ref, *refs):
    firsts, (before_hbm, out_hbm, piece_ref, sems) = refs[: len(slots)], refs[len(slots) :]
    size = late_ref.shape[1]
    stores = []
    for at, slot in enumerate(slots):
        source = place_ref[0] ^ slot
        piece_ref[at] = firsts[at][...] + late_ref[at]
        store = pltpu.make_async_copy(
            piece_ref.at[at],
            out_hbm.at[pl.ds(pl.multiple_of(source * size, size), size)],
            sems.at[at],
        )
        store.start()
        stores.append(store)
    for store in stores:
        store.wait()


SPACES = {"s": pltpu.SMEM, "v": pltpu.VMEM, "h": pltpu.HBM, "a": pl.ANY}


def kernel_call(body, shapes, spaces, flops, moved, limit, scratch=(), aliases=None):
    inputs, outputs = spaces.split(">")
    specs = [pl.BlockSpec(memory_space=SPACES[s]) for s in outputs]
    return pl.pallas_call(
        body,
        out_shape=shapes,
        in_specs=[pl.BlockSpec(memory_space=SPACES[s]) for s in inputs],
        out_specs=specs if isinstance(shapes, list) else specs[0],
        scratch_shapes=scratch,
        input_output_aliases=aliases or {},
        cost_estimate=pl.CostEstimate(flops=flops, bytes_accessed=moved, transcendentals=0),
        compiler_params=pltpu.CompilerParams(vmem_limit_bytes=limit * 2**20),
    )


def exchange(block, axis, distance):
    size = lax.axis_size(axis)
    return lax.ppermute(block, axis, [(i, i ^ distance) for i in range(size)])


def fast_path(u, v, ky_order, sizes, groups):
    planes, rows, slab, pens = sizes
    length_y = v.shape[1]
    group_rows = rows * pens
    length_z = group_rows * groups
    lanes = 128
    pen, group = lax.axis_index("pen"), lax.axis_index("grp")
    place = jnp.stack([pen, group]).astype(jnp.int32)
    order = ky_order[None, :]
    flops = 2 * 3 * planes * rows * length_y * length_y
    dma = pltpu.SemaphoreType.DMA
    field = pltpu.VMEM(v.shape, f32)
    tiles = slab // lanes
    recv = []
    for tile in range(tiles):
        v_blocks = kernel_call(
            functools.partial(second_kernel, sizes, tile),
            jax.ShapeDtypeStruct((pens, 2 * planes, rows, lanes), f32),
            "hh>h",
            flops // tiles,
            2**21,
            60,
            [
                pltpu.VMEM((1, length_y), jnp.int32),
                field,
                pltpu.VMEM((2, length_y // 4, length_y // tiles), bf16),
                pltpu.VMEM((pens // 2, 2 * planes, rows, lanes), f32),
                dma((pens + 2,)),
            ],
        )(order, v)
        v_blocks = v_blocks.reshape(groups * pens, rows, lanes)
        recv.append(lax.all_to_all(v_blocks, ("pen", "grp"), 0, 0, tiled=True))
    swap = jnp.asarray(np.eye(slab)[::-1].copy(), bf16)
    size = rows * 2 * planes * slab // lanes
    firsts = [None] * pens
    for slots in (SLOTS, [k for k in range(pens // 2) if k not in SLOTS]):
        if not slots:
            continue
        wide = len(slots) * slab
        pieces = kernel_call(
            functools.partial(first_kernel, sizes, slots),
            [jax.ShapeDtypeStruct((size, lanes), f32)] * (2 * len(slots)),
            "svvh>" + "h" * (2 * len(slots)),
            flops // pens * len(slots),
            2**21,
            60,
            [
                field,
                pltpu.VMEM((2, length_y // 4, 2 * wide), bf16),
                pltpu.VMEM((1, wide), jnp.int32),
                pltpu.VMEM((2 * len(slots), size, lanes), f32),
                dma((pens + 1,)),
            ],
        )(place, order, swap, u)
        for k, slot in enumerate(slots):
            firsts[slot], firsts[pens - 1 - slot] = pieces[2 * k], pieces[2 * k + 1]
    circulant = kernel_call(
        table_kernel,
        jax.ShapeDtypeStruct((2, 11, length_z // 8, length_z // 8), bf16),
        "a>v",
        2**24,
        2**21,
        16,
    )(firsts[pens // 2])
    arrived = {0: firsts[0]}
    for k in reversed(range(1, pens)):
        arrived[k] = exchange(firsts[k], "pen", k)
    flip = np.kron(np.eye(2), np.eye(lanes)[::-1])
    turn = jnp.where(pen >= pens // 2, jnp.asarray(flip, bf16), jnp.asarray(np.eye(2 * lanes), bf16))
    seconds = []
    for tile in range(tiles):
        parts = kernel_call(
            circulant_kernel,
            [jax.ShapeDtypeStruct((group_rows, lanes), f32)] * groups,
            "svvv>vvvv",
            3 * length_z * length_z * lanes,
            2**22,
            20,
        )(place, recv[tile], circulant, turn)
        seconds.append(parts[0])
        for k in range(1, groups):
            seconds.append(exchange(parts[k], "grp", k))
    slots = [k for k in range(pens) if k not in LAST]
    result, late = kernel_call(
        functools.partial(final_kernel, sizes, slots),
        [
            jax.ShapeDtypeStruct((pens * size, lanes), f32),
            jax.ShapeDtypeStruct((len(LAST), size, lanes), f32),
        ],
        "sv" + "v" * (len(slots) + groups * tiles) + ">hv",
        2**20,
        2**20,
        16,
        [pltpu.VMEM((len(slots), size, lanes), f32), dma((pens,))],
    )(place, order, *[arrived[k] for k in slots], *seconds)
    result = kernel_call(
        functools.partial(last_kernel, sorted(LAST)),
        jax.ShapeDtypeStruct(result.shape, f32),
        "sv" + "v" * len(LAST) + "h>h",
        2**18,
        2**18,
        8,
        [pltpu.VMEM((len(LAST), size, lanes), f32), dma((len(LAST),))],
        {2 + len(LAST): 0},
    )(place, late, *[arrived[k] for k in sorted(LAST)], result)
    result = result.reshape(group_rows, 2, tiles, planes, lanes)
    return jnp.transpose(result, (0, 1, 3, 2, 4)).reshape(group_rows, 2, planes, slab)


def whole_tables(length):
    half = length // 2
    n = lax.broadcasted_iota(jnp.int32, (half, half), 0) - lax.broadcasted_iota(
        jnp.int32, (half, half), 1
    )
    theta = 2.0 * math.pi / length * n.astype(f32)
    factor = jnp.where(n % 2 == 0, -1.0 / length, 1.0 / length)
    inverse = jnp.where(n == 0, 0.0, factor / jnp.where(n == 0, 1.0, jnp.sin(theta)))
    return jnp.cos(theta) * inverse, inverse


def plain_path(u, v, ky_order, sizes, groups):
    planes, rows, slab, pens = sizes
    length_y = v.shape[1]
    group_rows = rows * pens
    length_z = group_rows * groups
    half = length_y // 2
    exact = lax.Precision.HIGHEST
    pen = lax.axis_index("pen")
    upper = pen >= pens // 2
    waves = ky_order[:half]
    index = lax.iota(jnp.int32, length_y)[:, None]
    theta = 2.0 * math.pi / length_y * (index * waves[None, :] % length_y).astype(f32)
    mixed = 2.0 * math.pi / length_y * (index * (half - waves[None, :]) % length_y).astype(f32)
    special = (waves == 0) | (waves == half)
    sines = jnp.where(special, jnp.cos(mixed), jnp.sin(theta))
    both = 1.0 / math.sqrt(length_y) * jnp.stack([sines, jnp.cos(theta)])

    def transform(x):
        y = jnp.einsum("ry,pyk->prk", x, both, precision=exact)
        return y.reshape(2, planes, rows, pens // 2, slab)

    y = transform(v)
    y = jnp.concatenate([y, jnp.flip(y, 3)], 3)
    v_blocks = jnp.transpose(y, (3, 2, 0, 1, 4)).reshape(pens, rows, groups, -1)
    v_blocks = jnp.transpose(v_blocks, (2, 0, 1, 3)).reshape(groups * pens, rows, -1)
    y = transform(u) * signed_scale(waves, length_y).reshape(pens // 2, slab)
    turned = jnp.flip(y, (3, 4)) * jnp.array([1.0, -1.0], f32)[:, None, None, None, None]
    u_blocks = jnp.transpose(jnp.concatenate([y, turned], 3), (3, 2, 0, 1, 4))
    recv = lax.all_to_all(v_blocks, ("grp", "pen"), 0, 0, tiled=True).reshape(length_z, -1)
    u_recv = lax.all_to_all(u_blocks, "pen", 0, 0, tiled=True)
    table = whole_tables(length_z)
    top, bottom = recv[: length_z // 2], recv[length_z // 2 :]
    even = jnp.dot(table[0], top + bottom, precision=exact)
    odd = jnp.dot(table[1], top - bottom, precision=exact)
    deriv = jnp.concatenate([even + odd, even - odd], 0)
    back = lax.all_to_all(deriv.reshape(groups, group_rows, -1), "grp", 0, 0, tiled=True)
    back = jnp.transpose(back, (1, 0, 2)).reshape(group_rows, 2, planes, slab)
    back = jnp.where(upper, jnp.flip(back, 3), back)
    mine = lax.dynamic_slice_in_dim(ky_order, pen * slab, slab)
    special = (mine == 0) | (mine == half)
    s, c = back[:, 0], back[:, 1]
    first = jnp.where(special, 0.0, jnp.where(upper, s, -s))
    second = jnp.where(special & upper, -s, -c)
    return u_recv.reshape(group_rows, 2, planes, slab) + jnp.stack([first, second], 1)


def on_device(u_field, v_field, ky_order):
    planes, rows, length_y = u_field.shape
    pens, groups = lax.axis_size("pen"), lax.axis_size("grp")
    slab = length_y // pens
    u = u_field.reshape(planes * rows, length_y)
    v = v_field.reshape(planes * rows, length_y)
    fast = slab % 128 == 0 and rows % 8 == 0 and groups == 4 and planes == 2 and pens % 4 == 0
    fast = fast and length_y % 1024 == 0 and length_y & (length_y - 1) == 0 and pens & (pens - 1) == 0
    path = fast_path if fast else plain_path
    return path(u, v, ky_order, (planes, rows, slab, pens), groups)


def solution(mesh):
    placed = (P(None, ("grp", "pen"), None), P(None, ("grp", "pen"), None), P())

    return jax.shard_map(
        on_device,
        mesh=mesh,
        in_specs=placed,
        out_specs=P("grp", None, None, "pen"),
        check_vma=False,
    )
```

```python
import functools
import math

import jax
import jax.numpy as jnp
import numpy as np
from jax import lax
from jax.experimental import pallas as pl
from jax.experimental.pallas import tpu as pltpu
from jax.sharding import PartitionSpec as P


LAST = ((4, 0), (6, 1))
PARTS = {6: 2}
f32 = jnp.float32
bf16 = jnp.bfloat16


def split_two(x):
    high = x.astype(bf16)
    return high, (x - high.astype(f32)).astype(bf16)


def split_three(x):
    high = x.astype(bf16)
    rest = x - high.astype(f32)
    middle = rest.astype(bf16)
    return high, middle, (rest - middle.astype(f32)).astype(bf16)


def dot(a, b):
    return jnp.dot(a, b, preferred_element_type=f32)


def signed_scale(waves, length):
    signed = jnp.where(waves < length // 2, waves, waves - length)
    signed = jnp.where(waves == length // 2, 0, signed)
    return 2.0 / length * signed.astype(f32)


def cos_sin(residue, length):
    eighth = length // 8
    turned = (residue + eighth) & (length - 1)
    turn = turned // (2 * eighth)
    x = (2.0 * math.pi / length) * (turned - turn * (2 * eighth) - eighth).astype(f32)
    y = x * x
    cosine = 1.0 + y * (-1 / 2 + y * (1 / 24 + y * (-1 / 720 + y * (1 / 40320))))
    sine = x * (1.0 + y * (-1 / 6 + y * (1 / 120 + y * (-1 / 5040 + y * (1 / 362880)))))
    odd = (turn & 1) == 1
    first, second = jnp.where(odd, sine, cosine), jnp.where(odd, cosine, sine)
    return (
        jnp.where((turn == 1) | (turn == 2), -first, first),
        jnp.where(turn >= 2, -second, second),
    )


def reverse_lanes(x, swap):
    high, middle, low = split_three(x)
    return dot(high, swap) + (dot(middle, swap) + dot(low, swap))


def transform_block(fields, table_ref, waves, first, slab):
    field_high, field_low = fields
    rows = field_high.shape[0] // 4
    half = table_ref.shape[2] // 2
    sums = []
    for part in range(2):
        columns = pl.ds(part * half + first, slab)
        high, low = table_ref[0, :, columns], table_ref[1, :, columns]
        sums.append(dot(field_high, high) + (dot(field_high, low) + dot(field_low, high)))
    residue = waves & 3
    sign = jnp.where((residue & 1) == 1, -1.0, 1.0)
    cosine = jnp.where(residue == 0, 1.0, jnp.where(residue == 2, -1.0, 0.0))
    sine = jnp.where(residue == 1, 1.0, jnp.where(residue == 3, -1.0, 0.0))

    def folded(x):
        return (
            x[:rows] + sign * x[2 * rows : 3 * rows],
            x[rows : 2 * rows] + sign * x[3 * rows :],
        )

    even_c, odd_c = folded(sums[0])
    even_s, odd_s = folded(sums[1])
    return (
        even_c + cosine * odd_c - sine * odd_s,
        even_s + cosine * odd_s + sine * odd_c,
    )


def cut_pieces(slots):
    return [(k, part, PARTS.get(k, 1)) for k in slots for part in range(PARTS.get(k, 1))]


def fill_table(waves, table_ref, length):
    half = waves.shape[1]
    norm = 1.0 / math.sqrt(length)
    fine = 32
    coarse = length // 4 // fine
    special = (waves == 0) | (waves == length // 2)
    coarse_c, coarse_s = cos_sin(
        (fine * lax.broadcasted_iota(jnp.int32, (coarse, half), 0) * waves) & (length - 1), length
    )
    coarse_c, coarse_s = norm * coarse_c, norm * coarse_s
    index = lax.broadcasted_iota(jnp.int32, (fine, half), 0)
    fine_c, fine_s = cos_sin((index * waves) & (length - 1), length)
    other = norm * jnp.where((waves == 0) & ((index & 1) == 1), -1.0, 1.0)
    for a in range(coarse):
        this_c, this_s = coarse_c[a : a + 1], coarse_s[a : a + 1]
        here = slice(a * fine, (a + 1) * fine)
        cosines = this_c * fine_c - this_s * fine_s
        sines = this_c * fine_s + this_s * fine_c
        sines = jnp.where(special, other, sines)
        for part, values in enumerate((cosines, sines)):
            high, low = split_two(values)
            table_ref[0, here, part * half : (part + 1) * half] = high
            table_ref[1, here, part * half : (part + 1) * half] = low


def load_quarters(ref):
    quarter = ref.shape[1] // 4
    x = jnp.concatenate([ref[:, i * quarter : (i + 1) * quarter] for i in range(4)], 0)
    return split_two(x)


def second_kernel(
    sizes, tile, order_hbm, field_hbm, out_hbm, order_ref, field_ref, table_ref, piece_ref, sems
):
    planes, rows, slab, pens = sizes
    lanes = 128
    first_load = pltpu.make_async_copy(order_hbm, order_ref, sems.at[pens + 1])
    first_load.start()
    load = pltpu.make_async_copy(field_hbm, field_ref, sems.at[pens])
    load.start()
    first_load.wait()
    starts = [block * slab + tile * lanes for block in range(pens // 2)]
    waves = jnp.concatenate([order_ref[:, at : at + lanes] for at in starts], 1)
    fill_table(waves, table_ref, order_ref.shape[1])
    load.wait()
    fields = load_quarters(field_ref)
    copies = []
    for pair in range(pens // 4):
        first = 2 * pair * lanes
        here = waves[:, first : first + 2 * lanes]
        c, s = transform_block(fields, table_ref, here, first, 2 * lanes)
        for side in range(2):
            block = 2 * pair + side
            columns = slice(side * lanes, (side + 1) * lanes)
            for part, values in enumerate((s, c)):
                for plane in range(planes):
                    piece_ref[block, part * planes + plane] = values[
                        plane * rows : (plane + 1) * rows, columns
                    ]
            for target in (block, pens - 1 - block):
                copy = pltpu.make_async_copy(
                    piece_ref.at[block], out_hbm.at[target], sems.at[target]
                )
                copy.start()
                copies.append(copy)
    for copy in copies:
        copy.wait()


def first_kernel(sizes, slots, order_ref, swap_ref, field_hbm, *refs):
    planes, rows, slab, pens = sizes
    outs, (field_ref, table_ref, waves_ref, piece_ref, sems) = refs[:-5], refs[-5:]
    pieces = cut_pieces(range(pens))
    load = pltpu.make_async_copy(field_hbm, field_ref, sems.at[len(outs)])
    load.start()
    length = order_ref.shape[1]
    pen = lax.axis_index("pen")
    upper = pen >= pens // 2
    for i, slot in enumerate(slots):
        target = pen ^ slot
        block = jnp.where(upper, pens - 1 - target, target)
        first = pl.multiple_of(block * slab, slab)
        waves_ref[:, i * slab : (i + 1) * slab] = order_ref[:, pl.ds(first, slab)]
    fill_table(waves_ref[...], table_ref, length)
    load.wait()
    fields = load_quarters(field_ref)
    lanes = 128
    step = 2 * planes * (slab // lanes)
    copies = []
    for i in range(len(slots)):
        waves = waves_ref[:, i * slab : (i + 1) * slab]
        c, s = transform_block(fields, table_ref, waves, i * slab, slab)
        scale = signed_scale(waves, length)
        for part, values in enumerate((scale * s, scale * c)):
            turned = reverse_lanes(values, swap_ref[...])
            if part == 1:
                turned = -turned
            near, far = jnp.where(upper, turned, values), jnp.where(upper, values, turned)
            for to, piece in ((2 * i, near), (2 * i + 1, far)):
                for plane in range(planes):
                    for tile in range(slab // lanes):
                        at = (part * (slab // lanes) + tile) * planes + plane
                        piece_ref[to, pl.ds(at, rows, stride=step), :] = piece[
                            plane * rows : (plane + 1) * rows, tile * lanes : (tile + 1) * lanes
                        ]
        for to, slot in ((2 * i, slots[i]), (2 * i + 1, pens - 1 - slots[i])):
            for n, (other, part, parts) in enumerate(pieces):
                if other != slot:
                    continue
                height = rows * step // parts
                copy = pltpu.make_async_copy(
                    piece_ref.at[to, part * height : (part + 1) * height], outs[n], sems.at[n]
                )
                copy.start()
                copies.append(copy)
    for copy in copies:
        copy.wait()


def table_kernel(after_ref, out_ref):
    width = out_ref.shape[2]
    length = 8 * width
    rows = 64
    for distance in range(4):
        for at in range(0, width, rows):
            n = (
                lax.broadcasted_iota(jnp.int32, (rows, width), 0)
                - lax.broadcasted_iota(jnp.int32, (rows, width), 1)
                + (distance * width + at)
            )
            cosine, sine = cos_sin(n & (length - 1), length)
            factor = jnp.where((n & 1) == 1, 1.0 / length, -1.0 / length)
            inverse = jnp.where(n == 0, 0.0, factor / jnp.where(n == 0, 1.0, sine))
            here = slice(at, at + rows)
            for i, part in enumerate(split_two(cosine * inverse)):
                out_ref[i, distance, here, :] = part
            for i, part in enumerate(split_two(inverse)):
                out_ref[i, 4 + distance, here, :] = part
                if distance:
                    out_ref[i, 7 + distance, here, :] = -part


def circulant_kernel(recv_ref, table_ref, turn_ref, *out_refs):
    count, rows, lanes = recv_ref.shape
    width = count * rows // 8
    turn = turn_ref[...]
    top, bottom = [
        jnp.concatenate(
            [recv_ref[4 * pen + group] for group in groups for pen in range(count // 4)], 0
        )
        for groups in ((0, 1), (2, 3))
    ]

    def operand(x):
        return dot(jnp.concatenate(split_two(x), 1), turn).astype(bf16)

    plus, minus = operand(top + bottom), operand(top - bottom)
    for pair in range(2):
        group = lax.axis_index("grp") ^ pair
        swapped = group >= 2
        for i in range(2):
            row = 2 * (group & 1) + i

            def product(x, index):
                both = jnp.concatenate(
                    [
                        jnp.concatenate([table_ref[w, index(column)] for column in range(4)], 1)
                        for w in range(2)
                    ],
                    0,
                )
                both = dot(both, x)
                return both[:width, :lanes] + (both[:width, lanes:] + both[width:, :lanes])

            even = product(plus, lambda column: (row - column) & 3)
            odd = product(
                minus, lambda column: row - column + jnp.where(row >= column, 4, 11)
            )
            here = slice(i * width, (i + 1) * width)
            out_refs[pair][here, :] = even + jnp.where(swapped, -odd, odd)
            out_refs[pair + 2][here, :] = even + jnp.where(swapped, odd, -odd)


def final_kernel(sizes, early, late, order_ref, *refs):
    planes, rows, slab, pens = sizes
    lanes = 128
    tiles = slab // lanes
    step = 2 * planes * tiles
    count = 4 * tiles
    firsts, seconds = refs[: len(early)], refs[len(early) : len(early) + count]
    out_hbm, late_refs, (piece_ref, sems) = refs[-3 - len(late)], refs[-2 - len(late) : -2], refs[-2:]
    pen, group = lax.axis_index("pen"), lax.axis_index("grp")
    upper = pen >= pens // 2
    low_bit, high_bit = (group & 1) == 1, group >= 2
    waves = order_ref[:, pl.ds(pl.multiple_of(pen * slab, slab), slab)]
    specials = (waves == 0) | (waves == order_ref.shape[1] // 2)
    stores = []
    for at, (slot, part_at, parts) in enumerate([*early, *late]):
        source = pen ^ slot
        height = rows // parts
        first = pl.multiple_of(source * rows + part_at * height, height)
        is_early = at < len(early)
        r = [ref[pl.ds(first, height), :] for ref in seconds]
        r = [jnp.where(low_bit, r[k ^ 1], r[k]) for k in range(count)]
        r = [jnp.where(high_bit, r[k ^ 2], r[k]) for k in range(count)]
        if tiles == 2:
            r = [jnp.where(upper, r[k ^ 4], r[k]) for k in range(count)]
        for tile in range(tiles):
            special = specials[:, tile * lanes : (tile + 1) * lanes]
            base = 4 * tile
            for plane in range(planes):
                s, c = r[base + plane], r[base + planes + plane]
                pieces = (
                    jnp.where(special, 0.0, jnp.where(upper, s, -s)),
                    jnp.where(special & upper, -s, -c),
                )
                for part in range(2):
                    there = pl.ds((part * tiles + tile) * planes + plane, height, stride=step)
                    if is_early:
                        piece_ref[at, there, :] = firsts[at][there, :] + pieces[part]
                    else:
                        late_refs[at - len(early)][there, :] = pieces[part]
        if is_early:
            store = pltpu.make_async_copy(
                piece_ref.at[at, : height * step],
                out_hbm.at[pl.ds(first * step, height * step)],
                sems.at[at],
            )
            store.start()
            stores.append(store)
    for store in stores:
        store.wait()


def last_kernel(pieces, *refs):
    count = len(pieces)
    lates, firsts, (before_hbm, out_hbm, piece_ref, sems) = (
        refs[:count],
        refs[count : 2 * count],
        refs[2 * count :],
    )
    stores = []
    for at, (slot, part, parts) in enumerate(pieces):
        size = lates[at].shape[0]
        first = ((lax.axis_index("pen") ^ slot) * parts + part) * size
        piece_ref[at, :size] = firsts[at][...] + lates[at][...]
        store = pltpu.make_async_copy(
            piece_ref.at[at, :size],
            out_hbm.at[pl.ds(pl.multiple_of(first, size), size)],
            sems.at[at],
        )
        store.start()
        stores.append(store)
    for store in stores:
        store.wait()


SPACES = {"s": pltpu.SMEM, "v": pltpu.VMEM, "h": pltpu.HBM, "a": pl.ANY}


def kernel_call(body, shapes, spaces, flops, moved, limit, scratch=(), aliases=None):
    inputs, outputs = spaces.split(">")
    specs = [pl.BlockSpec(memory_space=SPACES[s]) for s in outputs]
    return pl.pallas_call(
        body,
        out_shape=shapes,
        in_specs=[pl.BlockSpec(memory_space=SPACES[s]) for s in inputs],
        out_specs=specs if isinstance(shapes, list) else specs[0],
        scratch_shapes=scratch,
        input_output_aliases=aliases or {},
        cost_estimate=pl.CostEstimate(flops=flops, bytes_accessed=moved, transcendentals=0),
        compiler_params=pltpu.CompilerParams(vmem_limit_bytes=limit * 2**20),
    )


def exchange(block, axis, distance):
    size = lax.axis_size(axis)
    return lax.ppermute(block, axis, [(i, i ^ distance) for i in range(size)])


def fast_path(u, v, ky_order, sizes, groups):
    planes, rows, slab, pens = sizes
    length_y = v.shape[1]
    group_rows = rows * pens
    length_z = group_rows * groups
    half = length_y // 2
    lanes = 128
    pen = lax.axis_index("pen")
    order = ky_order[None, :]
    flops = 2 * 3 * planes * rows * length_y * length_y
    dma = pltpu.SemaphoreType.DMA
    field = pltpu.VMEM(v.shape, f32)
    tiles = slab // lanes
    recv = []
    for tile in range(tiles):
        v_blocks = kernel_call(
            functools.partial(second_kernel, sizes, tile),
            jax.ShapeDtypeStruct((pens, 2 * planes, rows, lanes), f32),
            "hh>h",
            flops // tiles,
            2**21,
            60,
            [
                pltpu.VMEM((1, length_y), jnp.int32),
                field,
                pltpu.VMEM((2, length_y // 4, length_y // tiles), bf16),
                pltpu.VMEM((pens // 2, 2 * planes, rows, lanes), f32),
                dma((pens + 2,)),
            ],
        )(order, v)
        v_blocks = v_blocks.reshape(groups * pens, rows, lanes)
        recv.append(lax.all_to_all(v_blocks, ("pen", "grp"), 0, 0, tiled=True))
    swap = jnp.asarray(np.eye(slab)[::-1].copy(), bf16)
    size = rows * 2 * planes * slab // lanes
    pieces = cut_pieces(range(pens))
    half_pens = list(range(pens // 2))
    firsts = kernel_call(
        functools.partial(first_kernel, sizes, half_pens),
        [jax.ShapeDtypeStruct((size // parts, lanes), f32) for _, _, parts in pieces],
        "vvh>" + "h" * len(pieces),
        flops,
        2**21,
        60,
        [
            field,
            pltpu.VMEM((2, length_y // 4, length_y), bf16),
            pltpu.VMEM((1, half), jnp.int32),
            pltpu.VMEM((pens, size, lanes), f32),
            dma((len(pieces) + 1,)),
        ],
    )(order, swap, u)
    firsts = dict(zip(pieces, firsts))
    circulant = kernel_call(
        table_kernel,
        jax.ShapeDtypeStruct((2, 11, length_z // 8, length_z // 8), bf16),
        "a>v",
        2**24,
        2**21,
        16,
    )(firsts[pieces[0]])
    arrived = {}
    for piece in pieces:
        k, _, _ = piece
        arrived[piece] = exchange(firsts[piece], "pen", k) if k else firsts[piece]
    flip = np.kron(np.eye(2), np.eye(lanes)[::-1])
    turn = jnp.where(pen >= pens // 2, jnp.asarray(flip, bf16), jnp.asarray(np.eye(2 * lanes), bf16))
    seconds = []
    for tile in range(tiles):
        parts = kernel_call(
            circulant_kernel,
            [jax.ShapeDtypeStruct((group_rows, lanes), f32)] * groups,
            "vvv>vvvv",
            3 * length_z * length_z * lanes,
            2**22,
            20,
        )(recv[tile], circulant, turn)
        seconds.append(parts[0])
        for k in range(1, groups):
            seconds.append(exchange(parts[k], "grp", k))
    early = [piece for piece in pieces if piece[:2] not in LAST]
    late = [piece for piece in pieces if piece[:2] in LAST]
    late_shapes = [jax.ShapeDtypeStruct((size // parts, lanes), f32) for _, _, parts in late]
    result, *rest = kernel_call(
        functools.partial(final_kernel, sizes, early, late),
        [jax.ShapeDtypeStruct((pens * size, lanes), f32), *late_shapes],
        "v" + "v" * (len(early) + groups * tiles) + ">h" + "v" * len(late),
        2**20,
        2**20,
        16,
        [pltpu.VMEM((len(early), size, lanes), f32), dma((len(early),))],
    )(order, *[arrived[piece] for piece in early], *seconds)
    tall = max(shape.shape[0] for shape in late_shapes)
    result = kernel_call(
        functools.partial(last_kernel, late),
        jax.ShapeDtypeStruct(result.shape, f32),
        "v" * (2 * len(late)) + "h>h",
        2**18,
        2**18,
        8,
        [pltpu.VMEM((len(late), tall, lanes), f32), dma((len(late),))],
        {2 * len(late): 0},
    )(*rest, *[arrived[piece] for piece in late], result)
    result = result.reshape(group_rows, 2, tiles, planes, lanes)
    return jnp.transpose(result, (0, 1, 3, 2, 4)).reshape(group_rows, 2, planes, slab)


def whole_tables(length):
    half = length // 2
    n = lax.broadcasted_iota(jnp.int32, (half, half), 0) - lax.broadcasted_iota(
        jnp.int32, (half, half), 1
    )
    theta = 2.0 * math.pi / length * n.astype(f32)
    factor = jnp.where(n % 2 == 0, -1.0 / length, 1.0 / length)
    inverse = jnp.where(n == 0, 0.0, factor / jnp.where(n == 0, 1.0, jnp.sin(theta)))
    return jnp.cos(theta) * inverse, inverse


def plain_path(u, v, ky_order, sizes, groups):
    planes, rows, slab, pens = sizes
    length_y = v.shape[1]
    group_rows = rows * pens
    length_z = group_rows * groups
    half = length_y // 2
    exact = lax.Precision.HIGHEST
    pen = lax.axis_index("pen")
    upper = pen >= pens // 2
    waves = ky_order[:half]
    index = lax.iota(jnp.int32, length_y)[:, None]
    theta = 2.0 * math.pi / length_y * (index * waves[None, :] % length_y).astype(f32)
    mixed = 2.0 * math.pi / length_y * (index * (half - waves[None, :]) % length_y).astype(f32)
    special = (waves == 0) | (waves == half)
    sines = jnp.where(special, jnp.cos(mixed), jnp.sin(theta))
    both = 1.0 / math.sqrt(length_y) * jnp.stack([sines, jnp.cos(theta)])

    def transform(x):
        y = jnp.einsum("ry,pyk->prk", x, both, precision=exact)
        return y.reshape(2, planes, rows, pens // 2, slab)

    y = transform(v)
    y = jnp.concatenate([y, jnp.flip(y, 3)], 3)
    v_blocks = jnp.transpose(y, (3, 2, 0, 1, 4)).reshape(pens, rows, groups, -1)
    v_blocks = jnp.transpose(v_blocks, (2, 0, 1, 3)).reshape(groups * pens, rows, -1)
    y = transform(u) * signed_scale(waves, length_y).reshape(pens // 2, slab)
    turned = jnp.flip(y, (3, 4)) * jnp.array([1.0, -1.0], f32)[:, None, None, None, None]
    u_blocks = jnp.transpose(jnp.concatenate([y, turned], 3), (3, 2, 0, 1, 4))
    recv = lax.all_to_all(v_blocks, ("grp", "pen"), 0, 0, tiled=True).reshape(length_z, -1)
    u_recv = lax.all_to_all(u_blocks, "pen", 0, 0, tiled=True)
    table = whole_tables(length_z)
    top, bottom = recv[: length_z // 2], recv[length_z // 2 :]
    even = jnp.dot(table[0], top + bottom, precision=exact)
    odd = jnp.dot(table[1], top - bottom, precision=exact)
    deriv = jnp.concatenate([even + odd, even - odd], 0)
    back = lax.all_to_all(deriv.reshape(groups, group_rows, -1), "grp", 0, 0, tiled=True)
    back = jnp.transpose(back, (1, 0, 2)).reshape(group_rows, 2, planes, slab)
    back = jnp.where(upper, jnp.flip(back, 3), back)
    mine = lax.dynamic_slice_in_dim(ky_order, pen * slab, slab)
    special = (mine == 0) | (mine == half)
    s, c = back[:, 0], back[:, 1]
    first = jnp.where(special, 0.0, jnp.where(upper, s, -s))
    second = jnp.where(special & upper, -s, -c)
    return u_recv.reshape(group_rows, 2, planes, slab) + jnp.stack([first, second], 1)


def on_device(u_field, v_field, ky_order):
    planes, rows, length_y = u_field.shape
    pens, groups = lax.axis_size("pen"), lax.axis_size("grp")
    slab = length_y // pens
    u = u_field.reshape(planes * rows, length_y)
    v = v_field.reshape(planes * rows, length_y)
    fast = slab % 128 == 0 and rows % 8 == 0 and groups == 4 and planes == 2 and pens % 4 == 0
    fast = fast and length_y % 1024 == 0 and length_y & (length_y - 1) == 0 and pens & (pens - 1) == 0
    path = fast_path if fast else plain_path
    return path(u, v, ky_order, (planes, rows, slab, pens), groups)


def solution(mesh):
    placed = (P(None, ("grp", "pen"), None), P(None, ("grp", "pen"), None), P())

    return jax.shard_map(
        on_device,
        mesh=mesh,
        in_specs=placed,
        out_specs=P("grp", None, None, "pen"),
        check_vma=False,
    )
```

```python
import functools
import math

import jax
import jax.numpy as jnp
import numpy as np
from jax import lax
from jax.experimental import pallas as pl
from jax.experimental.pallas import tpu as pltpu
from jax.sharding import PartitionSpec as P


LAST = ((4, 0),)
PARTS = {6: 2}
SLOTS = (0,)
f32 = jnp.float32
bf16 = jnp.bfloat16


def split_two(x):
    high = x.astype(bf16)
    return high, (x - high.astype(f32)).astype(bf16)


def split_three(x):
    high = x.astype(bf16)
    rest = x - high.astype(f32)
    middle = rest.astype(bf16)
    return high, middle, (rest - middle.astype(f32)).astype(bf16)


def dot(a, b):
    return jnp.dot(a, b, preferred_element_type=f32)


def signed_scale(waves, length):
    signed = jnp.where(waves < length // 2, waves, waves - length)
    signed = jnp.where(waves == length // 2, 0, signed)
    return 2.0 / length * signed.astype(f32)


def cos_sin(residue, length):
    eighth = length // 8
    turned = (residue + eighth) & (length - 1)
    turn = turned // (2 * eighth)
    x = (2.0 * math.pi / length) * (turned - turn * (2 * eighth) - eighth).astype(f32)
    y = x * x
    cosine = 1.0 + y * (-1 / 2 + y * (1 / 24 + y * (-1 / 720 + y * (1 / 40320))))
    sine = x * (1.0 + y * (-1 / 6 + y * (1 / 120 + y * (-1 / 5040 + y * (1 / 362880)))))
    odd = (turn & 1) == 1
    first, second = jnp.where(odd, sine, cosine), jnp.where(odd, cosine, sine)
    return (
        jnp.where((turn == 1) | (turn == 2), -first, first),
        jnp.where(turn >= 2, -second, second),
    )


def reverse_lanes(x, swap):
    high, middle, low = split_three(x)
    return dot(high, swap) + (dot(middle, swap) + dot(low, swap))


def transform_block(fields, table_ref, waves, first, slab):
    field_high, field_low = fields
    rows = field_high.shape[0] // 4
    half = table_ref.shape[2] // 2
    sums = []
    for part in range(2):
        columns = pl.ds(part * half + first, slab)
        high, low = table_ref[0, :, columns], table_ref[1, :, columns]
        sums.append(dot(field_high, high) + (dot(field_high, low) + dot(field_low, high)))
    residue = waves & 3
    sign = jnp.where((residue & 1) == 1, -1.0, 1.0)
    cosine = jnp.where(residue == 0, 1.0, jnp.where(residue == 2, -1.0, 0.0))
    sine = jnp.where(residue == 1, 1.0, jnp.where(residue == 3, -1.0, 0.0))

    def folded(x):
        return (
            x[:rows] + sign * x[2 * rows : 3 * rows],
            x[rows : 2 * rows] + sign * x[3 * rows :],
        )

    even_c, odd_c = folded(sums[0])
    even_s, odd_s = folded(sums[1])
    return (
        even_c + cosine * odd_c - sine * odd_s,
        even_s + cosine * odd_s + sine * odd_c,
    )


def cut_pieces(slots):
    return [(k, part, PARTS.get(k, 1)) for k in slots for part in range(PARTS.get(k, 1))]


def fill_table(waves, table_ref, length):
    half = waves.shape[1]
    norm = 1.0 / math.sqrt(length)
    fine = 32
    coarse = length // 4 // fine
    special = (waves == 0) | (waves == length // 2)
    coarse_c, coarse_s = cos_sin(
        (fine * lax.broadcasted_iota(jnp.int32, (coarse, half), 0) * waves) & (length - 1), length
    )
    coarse_c, coarse_s = norm * coarse_c, norm * coarse_s
    index = lax.broadcasted_iota(jnp.int32, (fine, half), 0)
    fine_c, fine_s = cos_sin((index * waves) & (length - 1), length)
    other = norm * jnp.where((waves == 0) & ((index & 1) == 1), -1.0, 1.0)
    for a in range(coarse):
        this_c, this_s = coarse_c[a : a + 1], coarse_s[a : a + 1]
        here = slice(a * fine, (a + 1) * fine)
        cosines = this_c * fine_c - this_s * fine_s
        sines = this_c * fine_s + this_s * fine_c
        sines = jnp.where(special, other, sines)
        for part, values in enumerate((cosines, sines)):
            high, low = split_two(values)
            table_ref[0, here, part * half : (part + 1) * half] = high
            table_ref[1, here, part * half : (part + 1) * half] = low


def load_quarters(ref):
    quarter = ref.shape[1] // 4
    x = jnp.concatenate([ref[:, i * quarter : (i + 1) * quarter] for i in range(4)], 0)
    return split_two(x)


def second_kernel(
    sizes, tile, order_hbm, field_hbm, out_hbm, order_ref, field_ref, table_ref, piece_ref, sems
):
    planes, rows, slab, pens = sizes
    lanes = 128
    first_load = pltpu.make_async_copy(order_hbm, order_ref, sems.at[pens + 1])
    first_load.start()
    load = pltpu.make_async_copy(field_hbm, field_ref, sems.at[pens])
    load.start()
    first_load.wait()
    starts = [block * slab + tile * lanes for block in range(pens // 2)]
    waves = jnp.concatenate([order_ref[:, at : at + lanes] for at in starts], 1)
    fill_table(waves, table_ref, order_ref.shape[1])
    load.wait()
    fields = load_quarters(field_ref)
    copies = []
    for pair in range(pens // 4):
        first = 2 * pair * lanes
        here = waves[:, first : first + 2 * lanes]
        c, s = transform_block(fields, table_ref, here, first, 2 * lanes)
        for side in range(2):
            block = 2 * pair + side
            columns = slice(side * lanes, (side + 1) * lanes)
            for part, values in enumerate((s, c)):
                for plane in range(planes):
                    piece_ref[block, part * planes + plane] = values[
                        plane * rows : (plane + 1) * rows, columns
                    ]
            for target in (block, pens - 1 - block):
                copy = pltpu.make_async_copy(
                    piece_ref.at[block], out_hbm.at[target], sems.at[target]
                )
                copy.start()
                copies.append(copy)
    for copy in copies:
        copy.wait()


def first_kernel(sizes, slots, order_hbm, swap_hbm, field_hbm, *refs):
    planes, rows, slab, pens = sizes
    outs = refs[:-8]
    order_ref, swap_ref, field_ref, table_ref, waves_ref, piece_ref, load_sems, sems = refs[-8:]
    distances = [k for slot in slots for k in (slot, pens - 1 - slot)]
    pieces = cut_pieces(distances)
    loads = [
        pltpu.make_async_copy(*pair, load_sems.at[i])
        for i, pair in enumerate(
            ((order_hbm, order_ref), (field_hbm, field_ref), (swap_hbm, swap_ref))
        )
    ]
    for load in loads:
        load.start()
    loads[0].wait()
    length = order_ref.shape[1]
    pen = lax.axis_index("pen")
    upper = pen >= pens // 2
    for i, slot in enumerate(slots):
        target = pen ^ slot
        block = jnp.where(upper, pens - 1 - target, target)
        first = pl.multiple_of(block * slab, slab)
        waves_ref[:, i * slab : (i + 1) * slab] = order_ref[:, pl.ds(first, slab)]
    fill_table(waves_ref[...], table_ref, length)
    loads[1].wait()
    fields = load_quarters(field_ref)
    loads[2].wait()
    lanes = 128
    step = 2 * planes * (slab // lanes)
    copies = []
    for i in range(len(slots)):
        waves = waves_ref[:, i * slab : (i + 1) * slab]
        c, s = transform_block(fields, table_ref, waves, i * slab, slab)
        scale = signed_scale(waves, length)
        for part, values in enumerate((scale * s, scale * c)):
            turned = reverse_lanes(values, swap_ref[...])
            if part == 1:
                turned = -turned
            near, far = jnp.where(upper, turned, values), jnp.where(upper, values, turned)
            for to, piece in ((2 * i, near), (2 * i + 1, far)):
                for plane in range(planes):
                    for tile in range(slab // lanes):
                        at = (part * (slab // lanes) + tile) * planes + plane
                        piece_ref[to, pl.ds(at, rows, stride=step), :] = piece[
                            plane * rows : (plane + 1) * rows, tile * lanes : (tile + 1) * lanes
                        ]
        for to, slot in list(enumerate(distances))[2 * i : 2 * i + 2]:
            for n, (other, part, parts) in enumerate(pieces):
                if other != slot:
                    continue
                height = rows * step // parts
                copy = pltpu.make_async_copy(
                    piece_ref.at[to, part * height : (part + 1) * height], outs[n], sems.at[n]
                )
                copy.start()
                copies.append(copy)
    for copy in copies:
        copy.wait()


def table_kernel(after_ref, out_ref):
    width = out_ref.shape[2]
    length = 8 * width
    rows = 64
    for distance in range(4):
        for at in range(0, width, rows):
            n = (
                lax.broadcasted_iota(jnp.int32, (rows, width), 0)
                - lax.broadcasted_iota(jnp.int32, (rows, width), 1)
                + (distance * width + at)
            )
            cosine, sine = cos_sin(n & (length - 1), length)
            factor = jnp.where((n & 1) == 1, 1.0 / length, -1.0 / length)
            inverse = jnp.where(n == 0, 0.0, factor / jnp.where(n == 0, 1.0, sine))
            here = slice(at, at + rows)
            for i, part in enumerate(split_two(cosine * inverse)):
                out_ref[i, distance, here, :] = part
            for i, part in enumerate(split_two(inverse)):
                out_ref[i, 4 + distance, here, :] = part
                if distance:
                    out_ref[i, 7 + distance, here, :] = -part


def circulant_kernel(recv_ref, table_ref, turn_ref, *out_refs):
    count, rows, lanes = recv_ref.shape
    width = count * rows // 8
    turn = turn_ref[...]
    top, bottom = [
        jnp.concatenate(
            [recv_ref[4 * pen + group] for group in groups for pen in range(count // 4)], 0
        )
        for groups in ((0, 1), (2, 3))
    ]

    def operand(x):
        return dot(jnp.concatenate(split_two(x), 1), turn).astype(bf16)

    plus, minus = operand(top + bottom), operand(top - bottom)
    for pair in range(2):
        group = lax.axis_index("grp") ^ pair
        swapped = group >= 2
        for i in range(2):
            row = 2 * (group & 1) + i

            def product(x, index):
                both = jnp.concatenate(
                    [
                        jnp.concatenate([table_ref[w, index(column)] for column in range(4)], 1)
                        for w in range(2)
                    ],
                    0,
                )
                both = dot(both, x)
                return both[:width, :lanes] + (both[:width, lanes:] + both[width:, :lanes])

            even = product(plus, lambda column: (row - column) & 3)
            odd = product(
                minus, lambda column: row - column + jnp.where(row >= column, 4, 11)
            )
            here = slice(i * width, (i + 1) * width)
            out_refs[pair][here, :] = even + jnp.where(swapped, -odd, odd)
            out_refs[pair + 2][here, :] = even + jnp.where(swapped, odd, -odd)


def final_kernel(sizes, early, late, order_ref, *refs):
    planes, rows, slab, pens = sizes
    lanes = 128
    tiles = slab // lanes
    step = 2 * planes * tiles
    count = 4 * tiles
    firsts, seconds = refs[: len(early)], refs[len(early) : len(early) + count]
    out_hbm, late_refs, (piece_ref, sems) = refs[-3 - len(late)], refs[-2 - len(late) : -2], refs[-2:]
    pen, group = lax.axis_index("pen"), lax.axis_index("grp")
    upper = pen >= pens // 2
    low_bit, high_bit = (group & 1) == 1, group >= 2
    waves = order_ref[:, pl.ds(pl.multiple_of(pen * slab, slab), slab)]
    specials = (waves == 0) | (waves == order_ref.shape[1] // 2)
    stores = []
    for at, (slot, part_at, parts) in enumerate([*early, *late]):
        source = pen ^ slot
        height = rows // parts
        first = pl.multiple_of(source * rows + part_at * height, height)
        is_early = at < len(early)
        r = [ref[pl.ds(first, height), :] for ref in seconds]
        r = [jnp.where(low_bit, r[k ^ 1], r[k]) for k in range(count)]
        r = [jnp.where(high_bit, r[k ^ 2], r[k]) for k in range(count)]
        if tiles == 2:
            r = [jnp.where(upper, r[k ^ 4], r[k]) for k in range(count)]
        for tile in range(tiles):
            special = specials[:, tile * lanes : (tile + 1) * lanes]
            base = 4 * tile
            for plane in range(planes):
                s, c = r[base + plane], r[base + planes + plane]
                pieces = (
                    jnp.where(special, 0.0, jnp.where(upper, s, -s)),
                    jnp.where(special & upper, -s, -c),
                )
                for part in range(2):
                    there = pl.ds((part * tiles + tile) * planes + plane, height, stride=step)
                    if is_early:
                        piece_ref[at, there, :] = firsts[at][there, :] + pieces[part]
                    else:
                        late_refs[at - len(early)][there, :] = pieces[part]
        if is_early:
            store = pltpu.make_async_copy(
                piece_ref.at[at, : height * step],
                out_hbm.at[pl.ds(first * step, height * step)],
                sems.at[at],
            )
            store.start()
            stores.append(store)
    for store in stores:
        store.wait()


def last_kernel(pieces, *refs):
    count = len(pieces)
    lates, firsts, (before_hbm, out_hbm, piece_ref, sems) = (
        refs[:count],
        refs[count : 2 * count],
        refs[2 * count :],
    )
    stores = []
    for at, (slot, part, parts) in enumerate(pieces):
        size = lates[at].shape[0]
        first = ((lax.axis_index("pen") ^ slot) * parts + part) * size
        piece_ref[at, :size] = firsts[at][...] + lates[at][...]
        store = pltpu.make_async_copy(
            piece_ref.at[at, :size],
            out_hbm.at[pl.ds(pl.multiple_of(first, size), size)],
            sems.at[at],
        )
        store.start()
        stores.append(store)
    for store in stores:
        store.wait()


SPACES = {"s": pltpu.SMEM, "v": pltpu.VMEM, "h": pltpu.HBM, "a": pl.ANY}


def kernel_call(body, shapes, spaces, flops, moved, limit, scratch=(), aliases=None):
    inputs, outputs = spaces.split(">")
    specs = [pl.BlockSpec(memory_space=SPACES[s]) for s in outputs]
    return pl.pallas_call(
        body,
        out_shape=shapes,
        in_specs=[pl.BlockSpec(memory_space=SPACES[s]) for s in inputs],
        out_specs=specs if isinstance(shapes, list) else specs[0],
        scratch_shapes=scratch,
        input_output_aliases=aliases or {},
        cost_estimate=pl.CostEstimate(flops=flops, bytes_accessed=moved, transcendentals=0),
        compiler_params=pltpu.CompilerParams(vmem_limit_bytes=limit * 2**20),
    )


def exchange(block, axis, distance):
    size = lax.axis_size(axis)
    return lax.ppermute(block, axis, [(i, i ^ distance) for i in range(size)])


def fast_path(u, v, ky_order, sizes, groups):
    planes, rows, slab, pens = sizes
    length_y = v.shape[1]
    group_rows = rows * pens
    length_z = group_rows * groups
    lanes = 128
    pen = lax.axis_index("pen")
    order = ky_order[None, :]
    flops = 2 * 3 * planes * rows * length_y * length_y
    dma = pltpu.SemaphoreType.DMA
    field = pltpu.VMEM(v.shape, f32)
    tiles = slab // lanes
    recv = []
    for tile in range(tiles):
        v_blocks = kernel_call(
            functools.partial(second_kernel, sizes, tile),
            jax.ShapeDtypeStruct((pens, 2 * planes, rows, lanes), f32),
            "hh>h",
            flops // tiles,
            2**21,
            60,
            [
                pltpu.VMEM((1, length_y), jnp.int32),
                field,
                pltpu.VMEM((2, length_y // 4, length_y // tiles), bf16),
                pltpu.VMEM((pens // 2, 2 * planes, rows, lanes), f32),
                dma((pens + 2,)),
            ],
        )(order, v)
        v_blocks = v_blocks.reshape(groups * pens, rows, lanes)
        recv.append(lax.all_to_all(v_blocks, ("pen", "grp"), 0, 0, tiled=True))
    swap = jnp.asarray(np.eye(slab)[::-1].copy(), bf16)
    size = rows * 2 * planes * slab // lanes
    pieces = cut_pieces(range(pens))
    firsts = {}
    for slots in (SLOTS, [k for k in range(pens // 2) if k not in SLOTS]):
        wide = len(slots) * slab
        ours = cut_pieces([k for slot in slots for k in (slot, pens - 1 - slot)])
        values = kernel_call(
            functools.partial(first_kernel, sizes, slots),
            [jax.ShapeDtypeStruct((size // parts, lanes), f32) for _, _, parts in ours],
            "hhh>" + "h" * len(ours),
            flops // pens * len(slots),
            2**21,
            60,
            [
                pltpu.VMEM((1, length_y), jnp.int32),
                pltpu.VMEM((slab, slab), bf16),
                field,
                pltpu.VMEM((2, length_y // 4, 2 * wide), bf16),
                pltpu.VMEM((1, wide), jnp.int32),
                pltpu.VMEM((2 * len(slots), size, lanes), f32),
                dma((3,)),
                dma((len(ours),)),
            ],
        )(order, swap, u)
        firsts.update(zip(ours, values))
    circulant = kernel_call(
        table_kernel,
        jax.ShapeDtypeStruct((2, 11, length_z // 8, length_z // 8), bf16),
        "a>v",
        2**24,
        2**21,
        16,
    )(firsts[pieces[-2]])
    arrived = {}
    for piece in pieces:
        k, _, _ = piece
        arrived[piece] = exchange(firsts[piece], "pen", k) if k else firsts[piece]
    flip = np.kron(np.eye(2), np.eye(lanes)[::-1])
    turn = jnp.where(pen >= pens // 2, jnp.asarray(flip, bf16), jnp.asarray(np.eye(2 * lanes), bf16))
    seconds = []
    for tile in range(tiles):
        parts = kernel_call(
            circulant_kernel,
            [jax.ShapeDtypeStruct((group_rows, lanes), f32)] * groups,
            "vvv>vvvv",
            3 * length_z * length_z * lanes,
            2**22,
            20,
        )(recv[tile], circulant, turn)
        seconds.append(parts[0])
        for k in range(1, groups):
            seconds.append(exchange(parts[k], "grp", k))
    early = [piece for piece in pieces if piece[:2] not in LAST]
    late = [piece for piece in pieces if piece[:2] in LAST]
    late_shapes = [jax.ShapeDtypeStruct((size // parts, lanes), f32) for _, _, parts in late]
    result, *rest = kernel_call(
        functools.partial(final_kernel, sizes, early, late),
        [jax.ShapeDtypeStruct((pens * size, lanes), f32), *late_shapes],
        "v" + "v" * (len(early) + groups * tiles) + ">h" + "v" * len(late),
        2**20,
        2**20,
        16,
        [pltpu.VMEM((len(early), size, lanes), f32), dma((len(early),))],
    )(order, *[arrived[piece] for piece in early], *seconds)
    tall = max(shape.shape[0] for shape in late_shapes)
    result = kernel_call(
        functools.partial(last_kernel, late),
        jax.ShapeDtypeStruct(result.shape, f32),
        "v" * (2 * len(late)) + "h>h",
        2**18,
        2**18,
        8,
        [pltpu.VMEM((len(late), tall, lanes), f32), dma((len(late),))],
        {2 * len(late): 0},
    )(*rest, *[arrived[piece] for piece in late], result)
    result = result.reshape(group_rows, 2, tiles, planes, lanes)
    return jnp.transpose(result, (0, 1, 3, 2, 4)).reshape(group_rows, 2, planes, slab)


def whole_tables(length):
    half = length // 2
    n = lax.broadcasted_iota(jnp.int32, (half, half), 0) - lax.broadcasted_iota(
        jnp.int32, (half, half), 1
    )
    theta = 2.0 * math.pi / length * n.astype(f32)
    factor = jnp.where(n % 2 == 0, -1.0 / length, 1.0 / length)
    inverse = jnp.where(n == 0, 0.0, factor / jnp.where(n == 0, 1.0, jnp.sin(theta)))
    return jnp.cos(theta) * inverse, inverse


def plain_path(u, v, ky_order, sizes, groups):
    planes, rows, slab, pens = sizes
    length_y = v.shape[1]
    group_rows = rows * pens
    length_z = group_rows * groups
    half = length_y // 2
    exact = lax.Precision.HIGHEST
    pen = lax.axis_index("pen")
    upper = pen >= pens // 2
    waves = ky_order[:half]
    index = lax.iota(jnp.int32, length_y)[:, None]
    theta = 2.0 * math.pi / length_y * (index * waves[None, :] % length_y).astype(f32)
    mixed = 2.0 * math.pi / length_y * (index * (half - waves[None, :]) % length_y).astype(f32)
    special = (waves == 0) | (waves == half)
    sines = jnp.where(special, jnp.cos(mixed), jnp.sin(theta))
    both = 1.0 / math.sqrt(length_y) * jnp.stack([sines, jnp.cos(theta)])

    def transform(x):
        y = jnp.einsum("ry,pyk->prk", x, both, precision=exact)
        return y.reshape(2, planes, rows, pens // 2, slab)

    y = transform(v)
    y = jnp.concatenate([y, jnp.flip(y, 3)], 3)
    v_blocks = jnp.transpose(y, (3, 2, 0, 1, 4)).reshape(pens, rows, groups, -1)
    v_blocks = jnp.transpose(v_blocks, (2, 0, 1, 3)).reshape(groups * pens, rows, -1)
    y = transform(u) * signed_scale(waves, length_y).reshape(pens // 2, slab)
    turned = jnp.flip(y, (3, 4)) * jnp.array([1.0, -1.0], f32)[:, None, None, None, None]
    u_blocks = jnp.transpose(jnp.concatenate([y, turned], 3), (3, 2, 0, 1, 4))
    recv = lax.all_to_all(v_blocks, ("grp", "pen"), 0, 0, tiled=True).reshape(length_z, -1)
    u_recv = lax.all_to_all(u_blocks, "pen", 0, 0, tiled=True)
    table = whole_tables(length_z)
    top, bottom = recv[: length_z // 2], recv[length_z // 2 :]
    even = jnp.dot(table[0], top + bottom, precision=exact)
    odd = jnp.dot(table[1], top - bottom, precision=exact)
    deriv = jnp.concatenate([even + odd, even - odd], 0)
    back = lax.all_to_all(deriv.reshape(groups, group_rows, -1), "grp", 0, 0, tiled=True)
    back = jnp.transpose(back, (1, 0, 2)).reshape(group_rows, 2, planes, slab)
    back = jnp.where(upper, jnp.flip(back, 3), back)
    mine = lax.dynamic_slice_in_dim(ky_order, pen * slab, slab)
    special = (mine == 0) | (mine == half)
    s, c = back[:, 0], back[:, 1]
    first = jnp.where(special, 0.0, jnp.where(upper, s, -s))
    second = jnp.where(special & upper, -s, -c)
    return u_recv.reshape(group_rows, 2, planes, slab) + jnp.stack([first, second], 1)


def on_device(u_field, v_field, ky_order):
    planes, rows, length_y = u_field.shape
    pens, groups = lax.axis_size("pen"), lax.axis_size("grp")
    slab = length_y // pens
    u = u_field.reshape(planes * rows, length_y)
    v = v_field.reshape(planes * rows, length_y)
    fast = slab % 128 == 0 and rows % 8 == 0 and groups == 4 and planes == 2 and pens % 4 == 0
    fast = fast and length_y % 1024 == 0 and length_y & (length_y - 1) == 0 and pens & (pens - 1) == 0
    path = fast_path if fast else plain_path
    return path(u, v, ky_order, (planes, rows, slab, pens), groups)


def solution(mesh):
    placed = (P(None, ("grp", "pen"), None), P(None, ("grp", "pen"), None), P())

    return jax.shard_map(
        on_device,
        mesh=mesh,
        in_specs=placed,
        out_specs=P("grp", None, None, "pen"),
        check_vma=False,
    )
```
